32 devices in a mesh: grp: 2 (over x), seq: 16 (over z, y, core).
Axes of the slice: x: 2, y: 2, z: 4, core: 2. Of those that a mesh axis runs over, the one named last changes fastest.
Arguments:
- feats: bfloat16 [32, 128, 384], P('seq', None, 'grp'), may hold values from -6 to 6
- conv_weight: bfloat16 [3, 128, 128], replicated, may hold values from -0.3125 to 0.3125
- conv_bias: float32 [128], replicated, may hold values from -3 to 3
- latent_projection_weight: bfloat16 [16, 128], replicated, may hold values from -0.75 to 0.75
- noise: bfloat16 [32, 16, 384], P('seq', None, 'grp'), may hold values from -6 to 6
- step_index: int32 [1], replicated, may hold values from 0 to 49
- hist: bfloat16 [128, 64], P('seq'), may hold values from -6 to 6
- hist_level: int32 [128], P('seq'), may hold values from 0 to 2
- hist_count: int32 [16], replicated, may hold values from 1 to 8, 96 in all
- w_in: bfloat16 [64, 3072], replicated, may hold values from -2 to 2
- w_hist: bfloat16 [3, 64, 3072], replicated, may hold values from -0.75 to 0.75
- norm_gain: float32 [3072], replicated, may hold values from 0.5 to 2
- w_query: bfloat16 [3072, 1536], P(None, 'grp'), may hold values from -2 to 2
- w_key: bfloat16 [3072, 1536], P(None, 'grp'), may hold values from -2 to 2
- w_value: bfloat16 [3072, 1536], P(None, 'grp'), may hold values from -0.109375 to 0.109375
- q_gain: float32 [128], replicated, may hold values from 0.5 to 6
- k_gain: float32 [128], replicated, may hold values from 0.5 to 6
- w_out: bfloat16 [1536, 3072], P('grp'), may hold values from -0.5 to 0.5
Outputs:
- attention_out: bfloat16 [3072, 3072], P('seq', 'grp')
The draws below stay inside these ranges and needn't reach their ends.
Inputs may be any that keep to these rules, and one draw needn't show every extreme that they name: hist_count[s] of the 8 history slots of seq index s are live; the largest count is exactly 8.
All inputs are finite; a program needn't handle non-finite values.
Results may differ from the reference program's by a relative error of at most 0.0095.
The reference program's roundings to bfloat16 on the way count: a program that leaves them out, or rounds other values in their place, can miss the bound.
Values may be sent and summed in bfloat16 or wider, within the bound.
No kernel may reach another device: no remote copies, remote signals or barrier semaphores. Data moves between devices by JAX's collectives and lax.ppermute only.
A program may use at most 256 MiB of HBM per device.

```python
import math
import jax
import jax.numpy as jnp
import numpy as np
from jax import lax

D = 3072
HD = 128
LAT = 16
HEADS = 12
CV = 128
STEPS = 50
PIXW = 384
HROWS = 8
PATCH = 64
FRAMES = 32
TOKENS = 3072
HIST = 128
N_SEQ = 16


def query_matrix(key):
    base_draw = jax.random.normal(jax.random.fold_in(key, 101), (D, HEADS * HD), jnp.float32)
    return base_draw * D ** (-0.5)


def draw_w_query(key, part):
    return jnp.clip(query_matrix(key), -2.0, 2.0).astype(jnp.bfloat16)


def draw_w_key(key, part):
    fresh_part = jax.random.normal(jax.random.fold_in(key, 102), (D, HEADS * HD), jnp.float32) * D ** (-0.5)
    matrix = fresh_part
    return jnp.clip(matrix, -2.0, 2.0).astype(jnp.bfloat16)


def draw_w_in(key, part):
    matrix = jax.random.normal(jax.random.fold_in(key, 104), (PATCH, D), jnp.float32) * PATCH ** (-0.5)
    return jnp.clip(matrix, -2.0, 2.0).astype(jnp.bfloat16)


def gain_draw(key, salt):
    values = jnp.exp(jax.random.uniform(jax.random.fold_in(key, salt), (HD,), jnp.float32, math.log(0.5), math.log(4.0)))
    return values


def draw_q_gain(key, part):
    return gain_draw(key, 105)


def draw_k_gain(key, part):
    return gain_draw(key, 106)


def touch_ends(entries, stream_key, low, largest):
    longest = entries.shape.index(max(entries.shape))
    spots = []
    for shift in (0, 1):
        where = [jax.random.randint(jax.random.fold_in(stream_key, axis), (), 0, length) for axis, length in enumerate(entries.shape)]
        where[longest] = (where[longest] + shift) % entries.shape[longest]
        spots.append(tuple(where))
    return entries.at[spots[0]].set(low).at[spots[1]].set(largest)


def steps_of(own_key, extent, cuts, low, high):
    def one(position, blocks):
        steps = jax.random.uniform(jax.random.fold_in(jax.random.fold_in(own_key, 6), position), (blocks,), jnp.float32, low / len(cuts), high / len(cuts))
        return jnp.repeat(jnp.exp(steps), extent[position] // blocks).reshape((-1,) + (1,) * (len(extent) - position - 1))

    factor_of = one(*cuts[0])
    for cut in cuts[1:]:
        factor_of = factor_of * one(*cut)
    return factor_of


def length_profile(number_of, total, limit, skew):
    loads = [(1 << 20) // math.isqrt(standing ** skew) + 1 for standing in range(2, number_of + 1)]
    rest, given = total - limit - (number_of - 1), [1] * (number_of - 1)
    while rest > 0:
        movable = [i for i in range(number_of - 1) if given[i] < limit]
        pool, remaining = sum([loads[i] for i in movable]), rest
        for i in movable:
            addition = min(limit - given[i], max(1, remaining * loads[i] // pool), rest)
            given[i] = given[i] + addition
            rest = rest - addition
    return np.array([limit] + given)


def uneven(key, amount, total, reach, slope):
    if amount == 2:
        one = jax.random.randint(key, (), max(1, total - reach), min(reach, total - 1) + 1)
        return jnp.stack([one, total - one])
    tallies = jnp.asarray(length_profile(amount, total, reach, slope), jnp.int32)
    twos = (amount - 1) // 2
    donor, taker = tallies[1:1 + 2 * twos:2], tallies[2:2 + 2 * twos:2]
    slack = jnp.minimum(donor - 1, reach - taker)
    shifted = jax.random.randint(jax.random.fold_in(key, 1), (twos,), 0, 1 << 20) % (slack + 1)
    tallies = tallies.at[1:1 + 2 * twos:2].set(donor - shifted).at[2:2 + 2 * twos:2].set(taker + shifted)
    return tallies[jax.random.permutation(jax.random.fold_in(key, 2), amount)]


def scatter_about(key, shape, scale, limit, pieces=(), kind=jnp.bfloat16):
    level = steps_of(key, shape, pieces, -0.22, 0.18) if pieces else 1.0
    values = jax.random.normal(key, shape, jnp.float32) * scale * level
    return jnp.minimum(jnp.maximum(values, -limit), limit).astype(kind)


def setup_inputs(seed: int = 0) -> dict:
    splits = jax.random.split(jax.random.key(seed), 19)
    feats = scatter_about(splits[0], (FRAMES, CV, PIXW), 1.0, 6.0, ((0, 16), (2, 2)))
    conv_weight = scatter_about(splits[1], (3, CV, CV), (3 * CV) ** -0.5, 0.3125)
    conv_bias = scatter_about(splits[2], (CV,), 0.5, 3.0, (), jnp.float32)
    latent_projection_weight = scatter_about(splits[3], (LAT, CV), (CV // 2) ** -0.5, 0.75)
    noise = scatter_about(splits[4], (FRAMES, LAT, PIXW), 1.0, 6.0, ((0, 16), (2, 2)))
    step_index = jax.random.randint(splits[5], (1,), 0, STEPS).astype(jnp.int32)
    hist = scatter_about(splits[6], (HIST, PATCH), 1.0, 6.0, ((0, 16),))
    hist_level = touch_ends(jax.random.randint(splits[7], (HIST,), 0, 3), jax.random.fold_in(splits[7], 1), 0, 2).astype(jnp.int32)
    hist_count = uneven(splits[8], N_SEQ, N_SEQ * HROWS * 3 // 4, HROWS, 2).astype(jnp.int32)
    w_in = draw_w_in(jax.random.fold_in(splits[18], 71), 0)
    w_hist = scatter_about(splits[10], (3, PATCH, D), PATCH ** -0.5, 0.75)
    norm_gain = jnp.clip(jnp.exp(jax.random.uniform(splits[11], (D,), jnp.float32, math.log(0.5), math.log(2.0))), 0.5, 2.0)
    w_query = draw_w_query(jax.random.fold_in(splits[18], 71), 0)
    w_key = draw_w_key(jax.random.fold_in(splits[18], 71), 0)
    w_value = scatter_about(splits[14], (D, HEADS * HD), D ** -0.5, 0.109375, ((1, 2),))
    q_gain = draw_q_gain(jax.random.fold_in(splits[18], 71), 0)
    k_gain = draw_k_gain(jax.random.fold_in(splits[18], 71), 0)
    w_out = scatter_about(splits[17], (HEADS * HD, D), HD ** -0.5, 0.5, ((0, 2),))
    return {"feats": feats, "conv_weight": conv_weight, "conv_bias": conv_bias, "latent_projection_weight": latent_projection_weight, "noise": noise, "step_index": step_index, "hist": hist, "hist_level": hist_level, "hist_count": hist_count, "w_in": w_in, "w_hist": w_hist, "norm_gain": norm_gain, "w_query": w_query, "w_key": w_key, "w_value": w_value, "q_gain": q_gain, "k_gain": k_gain, "w_out": w_out}


EPSILON = 1e-06

def time_embed(step_index, width):
    half_width = width // 2
    frequency = jnp.exp(-math.log(10000.0) * jnp.arange(half_width, dtype=jnp.float32) / half_width)
    angles = step_index[0].astype(jnp.float32) * frequency
    return jnp.concatenate([jnp.cos(angles), jnp.sin(angles)])

def rms_scale(values, gain):
    return values * lax.rsqrt(lax.optimization_barrier(jnp.mean(values * values, axis=-1, keepdims=True)) + EPSILON) * gain

def encode_video_section(feats, conv_weight, conv_bias, latent_projection_weight, noise, sigma):
    frame_count = feats.shape[0]
    padded = jnp.concatenate([jnp.zeros((2,) + feats.shape[1:], feats.dtype), feats], axis=0)
    total = jnp.zeros(feats.shape, jnp.float32)
    for tap_index in range(3):
        window = padded[2 - tap_index:2 - tap_index + frame_count]
        total = total + jnp.einsum('oc,tcp->top', conv_weight[tap_index].astype(jnp.float32), window.astype(jnp.float32))
    hidden_state = jax.nn.silu(total + conv_bias.astype(jnp.float32)[None, :, None]).astype(jnp.bfloat16)
    latent_input = jnp.einsum('qb,zby->zqy', latent_projection_weight.astype(jnp.float32), hidden_state.astype(jnp.float32))
    noisy = ((1.0 - sigma) * latent_input + sigma * noise.astype(jnp.float32)).astype(jnp.bfloat16)
    channels = noisy.shape[1]
    pixels = noisy.shape[2]
    return noisy.reshape(frame_count, channels, pixels // 4, 4).transpose(0, 2, 1, 3).reshape(frame_count * (pixels // 4), channels * 4)

def reference(feats, conv_weight, conv_bias, latent_projection_weight, noise, step_index, hist, hist_level, hist_count, w_in, w_hist, norm_gain, w_query, w_key, w_value, q_gain, k_gain, w_out):
    sigma = (STEPS - step_index[0].astype(jnp.float32)) / STEPS
    patches = encode_video_section(feats, conv_weight, conv_bias, latent_projection_weight, noise, sigma)
    embed = time_embed(step_index, D)
    gain = norm_gain.astype(jnp.float32)
    tokens = rms_scale(jnp.dot(patches, w_in, preferred_element_type=jnp.float32) + embed, gain).astype(jnp.bfloat16)
    history = jnp.zeros((HIST, D), jnp.float32)
    for level in range(3):
        history = history + jnp.dot(hist, w_hist[level], preferred_element_type=jnp.float32) * (hist_level == level).astype(jnp.float32)[:, None]
    history = rms_scale(history, gain).astype(jnp.bfloat16)
    both_rows = jnp.concatenate([tokens, history], axis=0)
    key_total = TOKENS + HIST
    query = rms_scale(jnp.dot(tokens, w_query, preferred_element_type=jnp.float32).reshape(TOKENS, HEADS, HD), q_gain.astype(jnp.float32)).astype(jnp.bfloat16)
    keys = rms_scale(jnp.dot(both_rows, w_key, preferred_element_type=jnp.float32).reshape(key_total, HEADS, HD), k_gain.astype(jnp.float32)).astype(jnp.bfloat16)
    values = jnp.dot(both_rows, w_value, preferred_element_type=jnp.float32).astype(jnp.bfloat16).reshape(key_total, HEADS, HD)
    slot_index = jnp.arange(HIST, dtype=jnp.int32)
    alive = jnp.concatenate([jnp.ones((TOKENS,), dtype=bool), slot_index % HROWS < jnp.repeat(hist_count, HROWS)])
    scale = 1.0 / math.sqrt(HD)

    def one_head(operands):
        q_head, k_head, v_head = operands
        scores = jnp.dot(q_head, k_head.T, preferred_element_type=jnp.float32) * scale
        scores = jnp.where(alive[None, :], scores, -1e+30)
        row_max = lax.optimization_barrier(jnp.max(scores, axis=1, keepdims=True))
        soft = jnp.where(alive[None, :], jnp.exp(scores - row_max), 0.0)
        row_sum = lax.optimization_barrier(jnp.sum(soft, axis=1, keepdims=True))
        return (jnp.dot(soft.astype(jnp.bfloat16), v_head, preferred_element_type=jnp.float32) / row_sum).astype(jnp.bfloat16)
    heads_out = lax.map(one_head, (query.transpose(1, 0, 2), keys.transpose(1, 0, 2), values.transpose(1, 0, 2)))
    merged = heads_out.transpose(1, 0, 2).reshape(TOKENS, HEADS * HD)
    return jnp.dot(merged, w_out, preferred_element_type=jnp.float32).astype(jnp.bfloat16)
```

```python
import functools
import math

import jax
import jax.numpy as jnp
from jax import lax
from jax.experimental import pallas as pl
from jax.experimental.pallas import tpu as pltpu
from jax.sharding import PartitionSpec as P

STEPS = 50
EPSILON = 1e-06
F32 = jnp.float32
BF16 = jnp.bfloat16
VMEM = pl.BlockSpec(memory_space=pltpu.VMEM)
SMEM = pl.BlockSpec(memory_space=pltpu.SMEM)


def dot(a, b):
    return jnp.dot(a, b, preferred_element_type=F32)


def time_embed(step_index, width):
    half_width = width // 2
    frequency = jnp.exp(-math.log(10000.0) * jnp.arange(half_width, dtype=F32) / half_width)
    angles = step_index[0].astype(F32) * frequency
    return jnp.concatenate([jnp.cos(angles), jnp.sin(angles)])


def encode_kernel(
    step_ref, feats_ref, earlier_ref, weight_ref, bias_ref, latent_ref, noise_ref, hist_ref,
    level_ref, out_ref,
):
    frames, channels, pixels = feats_ref.shape
    lat = noise_ref.shape[1]
    patch = lat * 4
    cells = pixels // 4
    diagonal = lax.broadcasted_iota(jnp.int32, (channels, channels), 0) == lax.broadcasted_iota(
        jnp.int32, (channels, channels), 1
    )
    bias = jnp.sum(jnp.where(diagonal, bias_ref[...], 0.0), axis=1, keepdims=True)
    step = jnp.full((lat, pixels), step_ref[0].astype(F32), F32)
    sigma = (STEPS - step) / STEPS
    row = lax.broadcasted_iota(jnp.int32, (lat, frames * patch), 0)
    lane = lax.broadcasted_iota(jnp.int32, (lat, frames * patch), 1)
    pixel = lax.broadcasted_iota(jnp.int32, (pixels, frames * patch), 0)
    feature = lax.broadcasted_iota(jnp.int32, (pixels, frames * patch), 1)
    keep = (pixel % 4) == (feature % 4)
    collect = (
        lax.broadcasted_iota(jnp.int32, (cells, pixels), 1) // 4
        == lax.broadcasted_iota(jnp.int32, (cells, pixels), 0)
    ).astype(BF16)
    patches = jnp.zeros((cells, frames * patch), F32)
    for t in range(frames):
        total = jnp.zeros((channels, pixels), F32)
        for tap in range(3):
            source = t - tap
            window = feats_ref[source] if source >= 0 else earlier_ref[frames + source]
            total = total + dot(weight_ref[tap], window)
        total = total + bias
        hidden = (total / (1.0 + jnp.exp(-total))).astype(BF16)
        mixed = dot(latent_ref[...], hidden)
        noisy = ((1.0 - sigma) * mixed + sigma * noise_ref[t].astype(F32)).astype(BF16)
        spread = (lane // 4 == row + t * lat).astype(BF16)
        wide = lax.dot_general(noisy, spread, (((0,), (0,)), ((), ())), preferred_element_type=F32)
        wide = jnp.where(keep, wide, 0.0).astype(BF16)
        patches = patches + dot(collect, wide)
    out_ref[0:cells, :] = patches.astype(BF16)
    slots = hist_ref.shape[0]
    level = jnp.broadcast_to(level_ref[...], (slots, patch)).astype(F32)
    tail = jnp.concatenate([hist_ref[...].astype(F32), level], axis=1)
    tail = jnp.concatenate([tail, jnp.zeros((out_ref.shape[0] - cells - slots, 2 * patch), F32)], axis=0)
    out_ref[cells:, :] = tail.astype(BF16)


def joint_kernel(
    info_ref, near_ref, far_ref, w_in_ref, w_hist_ref, embed_ref, gain_ref, w_q_ref, w_kv_ref,
    q_gain_ref, k_gain_ref, bias_ref, own_ref, sib_ref,
    patch_ref, hist_ref, x_ref, tok_ref, q_ref, k_ref, v_ref, s_ref,
    *, cells, slots, block, group_at, query_rows,
):
    heads, keys, size = k_ref.shape
    width = w_in_ref.shape[1]
    lanes = near_ref.shape[1]
    patch = w_in_ref.shape[0]
    half = near_ref.shape[0] // block
    tile = 4 * cells
    group = info_ref[0]
    hist_rows = hist_ref.shape[0]

    spot = 0
    for source in (near_ref, far_ref):
        for side in range(2):
            at = jnp.where(group == side, 0, group_at)
            patch_ref[spot * cells : (spot + 1) * cells, :] = source[
                pl.ds(pl.multiple_of(at * block, block), cells), :
            ]
            spot += 1
    for number, source in enumerate((near_ref, far_ref)):
        for p in range(half):
            if p != 0 and p != group_at:
                patch_ref[spot * cells : (spot + 1) * cells, :] = source[p * block : p * block + cells, :]
                spot += 1
        owners = group_at
        for p in range(owners):
            r = (number * owners + p) * slots
            hist_ref[r : r + slots, :] = source[p * block + cells : p * block + cells + slots, :].astype(F32)

    step = 512
    fold = 128

    def normalise(rows, with_embed, products):
        squares = jnp.zeros((rows, fold), F32)
        for n in range(0, width, step):
            x = products(n)
            if with_embed:
                x = x + embed_ref[:, n : n + step]
            x_ref[0:rows, n : n + step] = x
            for m in range(0, step, fold):
                part = x[:, m : m + fold]
                squares = squares + part * part
        mean = jnp.sum(squares, axis=1, keepdims=True) / width
        inverse = lax.rsqrt(mean + EPSILON)
        return inverse

    def emit(rows, at, inverse):
        for n in range(0, width, step):
            tok_ref[at : at + rows, n : n + step] = (
                x_ref[0:rows, n : n + step] * inverse * gain_ref[:, n : n + step]
            ).astype(BF16)

    def head_norm(values, gain):
        mean = jnp.mean(values * values, axis=1, keepdims=True)
        return (values * lax.rsqrt(mean + EPSILON) * gain).astype(BF16)

    def project(rows, at):
        both = dot(tok_ref[0:rows, :], w_kv_ref[...])
        for h in range(heads):
            k_ref[h, pl.ds(at, rows), :] = head_norm(both[:, h * size : (h + 1) * size], k_gain_ref[...])
            v_ref[h, pl.ds(at, rows), :] = both[:, (heads + h) * size : (heads + h + 1) * size].astype(BF16)

    tiles = patch_ref.shape[0] // tile
    frames = lanes // patch

    def token_tile(i, carry):
        source = patch_ref[pl.ds(pl.multiple_of(i * tile, tile), tile), :]
        for t in range(frames):
            part = source[:, t * patch : (t + 1) * patch]
            inverse = normalise(tile, True, lambda n: dot(part, w_in_ref[:, n : n + step]))
            emit(tile, t * tile, inverse)
        project(frames * tile, pl.multiple_of(i * (frames * tile), frames * tile))

        @pl.when(i == 0)
        def _():
            q = dot(tok_ref[...], w_q_ref[...])
            for h in range(heads):
                q_ref[h] = head_norm(q[:, h * size : (h + 1) * size], q_gain_ref[...])

        return carry

    lax.fori_loop(0, tiles, token_tile, 0)

    section = tiles * frames * tile
    for r in range(0, hist_rows, 128):
        rows = min(128, hist_rows - r)
        source = hist_ref[r : r + rows, :]
        values = source[:, 0:patch]
        level = source[:, patch : 2 * patch]
        parts = [jnp.where(level == v, values, 0.0).astype(BF16) for v in range(w_hist_ref.shape[0])]

        def products(n):
            total = dot(parts[0], w_hist_ref[0, :, n : n + step])
            for v in range(1, len(parts)):
                total = total + dot(parts[v], w_hist_ref[v, :, n : n + step])
            return total

        inverse = normalise(rows, False, products)
        emit(rows, 0, inverse)
        project(rows, section + r)

    scale = math.log2(math.e) / math.sqrt(size)
    chunk = 512
    pieces = [(a, chunk, False) for a in range(0, section, chunk)]
    pieces += [(section + r, min(128, hist_rows - r), True) for r in range(0, hist_rows, 128)]

    def attend(h, carry):
        for a in range(0, q_ref.shape[1], query_rows):
            q = q_ref[h, a : a + query_rows, :]
            top = jnp.full((query_rows, fold), -3e38, F32)
            for at, length, masked in pieces:
                s = lax.dot_general(
                    q, k_ref[h, at : at + length, :], (((1,), (1,)), ((), ())), preferred_element_type=F32
                )
                if masked:
                    s = s + bias_ref[:, at - section : at - section + length]
                s_ref[:, at : at + length] = s
                for m in range(0, length, fold):
                    top = jnp.maximum(top, s[:, m : m + fold])
            top = jnp.max(top, axis=1, keepdims=True)
            total = jnp.zeros((query_rows, fold), F32)
            weighted = jnp.zeros((query_rows, size), F32)
            for at, length, masked in pieces:
                soft = jnp.exp2((s_ref[:, at : at + length] - top) * scale)
                for m in range(0, length, fold):
                    total = total + soft[:, m : m + fold]
                weighted = weighted + dot(soft.astype(BF16), v_ref[h, at : at + length, :])
            out = (weighted / jnp.sum(total, axis=1, keepdims=True)).astype(BF16)
            q_ref[h, a : a + query_rows, :] = out
        return carry

    lax.fori_loop(0, heads, attend, 0)
    part = 2 * cells
    for h in range(heads):
        for t in range(frames):
            base = t * tile
            own_ref[t * part : (t + 1) * part, h * size : (h + 1) * size] = q_ref[h, base : base + part, :]
            sib_ref[t * part : (t + 1) * part, h * size : (h + 1) * size] = q_ref[
                h, base + part : base + tile, :
            ]


def combine_kernel(
    info_ref, own_ref, sib_ref, across_ref, corner_ref, w_local_ref, w_across_ref, w_corner_ref, out_ref
):
    core = info_ref[1]
    depth = own_ref.shape[1]
    mine = pl.ds(pl.multiple_of(core * depth, depth), depth)
    other = pl.ds(pl.multiple_of((1 - core) * depth, depth), depth)
    step = 512
    for n in range(0, out_ref.shape[1], step):
        columns = slice(n, n + step)
        total = dot(own_ref[...], w_local_ref[mine, columns])
        total = total + dot(sib_ref[...], w_local_ref[other, columns])
        total = total + dot(across_ref[...], w_across_ref[:, columns])
        total = total + dot(corner_ref[...], w_corner_ref[:, columns])
        out_ref[:, columns] = total.astype(BF16)


def flip(value, mask, seq_count):
    pairs = [(i, i ^ mask) for i in range(2 * seq_count)]
    return lax.ppermute(value, ("grp", "seq"), pairs)


def local(
    feats, conv_weight, conv_bias, latent_projection_weight, noise, step_index, hist, hist_level,
    hist_count, w_in, w_hist, norm_gain, w_query, w_key, w_value, q_gain, k_gain, w_out,
):
    frame_count, channels, pixels = feats.shape
    seq_count = lax.axis_size("seq")
    group = lax.axis_index("grp")
    place = lax.axis_index("seq")
    core = place % 2
    width = w_in.shape[1]
    patch = w_in.shape[0]
    cells = pixels // 4
    slots = hist.shape[0]
    block = cells + 16
    lanes = frame_count * patch
    size = q_gain.shape[0]
    heads = w_query.shape[1] // size // 2
    depth = heads * size

    earlier = lax.ppermute(feats, "seq", [(i, i + 1) for i in range(seq_count - 1)])
    gathered = pl.pallas_call(
        encode_kernel,
        out_shape=jax.ShapeDtypeStruct((block, lanes), BF16),
        in_specs=[SMEM] + [VMEM] * 8,
        out_specs=VMEM,
        name="encode",
    )(
        step_index, feats, earlier, conv_weight, conv_bias.reshape(1, channels),
        latent_projection_weight, noise, hist, hist_level.reshape(slots, 1),
    )

    masks = []
    bit = seq_count // 2
    while bit > 1:
        masks.append(bit)
        bit //= 2
    owner_masks = [0]
    for mask in masks:
        owner_masks = owner_masks + [m ^ mask for m in owner_masks]
    for mask in masks + [seq_count]:
        gathered = jnp.concatenate([gathered, flip(gathered, mask, seq_count)], axis=0)
    far = flip(gathered, 1, seq_count)
    group_at = len(owner_masks)

    owner = place ^ jnp.array(owner_masks + [m ^ 1 for m in owner_masks], jnp.int32)
    shards = jnp.arange(seq_count, dtype=jnp.int32)
    live = jnp.sum(jnp.where(owner[:, None] == shards[None, :], hist_count[None, :], 0), axis=1)
    slot = jnp.arange(slots, dtype=jnp.int32)
    bias = jnp.where(slot[None, :] < live[:, None], 0.0, -1e30).astype(F32).reshape(1, -1)

    w_q = lax.dynamic_slice_in_dim(w_query, core * depth, depth, axis=1)
    w_kv = jnp.concatenate(
        [
            lax.dynamic_slice_in_dim(w_key, core * depth, depth, axis=1),
            lax.dynamic_slice_in_dim(w_value, core * depth, depth, axis=1),
        ],
        axis=1,
    )
    columns = w_out.shape[1] // 2
    w_send = lax.dynamic_slice(w_out, (core * depth, (1 - group) * columns), (depth, columns))
    w_send, near = lax.optimization_barrier((w_send, gathered))
    w_across = flip(w_send, seq_count, seq_count)
    w_corner = flip(w_across, 1, seq_count)
    w_local = lax.dynamic_slice_in_dim(w_out, group * columns, columns, axis=1)

    info = jnp.stack([group, core]).astype(jnp.int32)
    hist_rows = slots * seq_count
    tokens = 2 * seq_count * frame_count * cells
    keys = tokens + hist_rows
    rows = frame_count * 4 * cells
    query_rows = rows if rows * keys * 4 <= 6 * 2**20 else rows // 2
    own, sib = pl.pallas_call(
        functools.partial(
            joint_kernel, cells=cells, slots=slots, block=block, group_at=group_at,
            query_rows=query_rows,
        ),
        out_shape=[jax.ShapeDtypeStruct((rows // 2, depth), BF16)] * 2,
        in_specs=[SMEM] + [VMEM] * 11,
        out_specs=[VMEM] * 2,
        scratch_shapes=[
            pltpu.VMEM((tokens // frame_count, lanes), BF16),
            pltpu.VMEM((hist_rows, lanes), F32),
            pltpu.VMEM((4 * cells, width), F32),
            pltpu.VMEM((rows, width), BF16),
            pltpu.VMEM((heads, rows, size), BF16),
            pltpu.VMEM((heads, keys, size), BF16),
            pltpu.VMEM((heads, keys, size), BF16),
            pltpu.VMEM((query_rows, keys), F32),
        ],
        compiler_params=pltpu.CompilerParams(vmem_limit_bytes=60 * 2**20),
        cost_estimate=pl.CostEstimate(
            flops=2 * keys * width * 3 * depth + 4 * rows * keys * depth,
            bytes_accessed=6 * width * depth,
            transcendentals=rows * keys * heads,
        ),
        name="joint",
    )(
        info, near, far, w_in, w_hist, time_embed(step_index, width).reshape(1, width),
        norm_gain.reshape(1, width), w_q, w_kv, q_gain.reshape(1, size), k_gain.reshape(1, size), bias,
    )
    from_sib = flip(sib, 1, seq_count)
    across = flip(own, seq_count, seq_count)
    corner = flip(sib, seq_count + 1, seq_count)
    return pl.pallas_call(
        combine_kernel,
        out_shape=jax.ShapeDtypeStruct((rows // 2, columns), BF16),
        in_specs=[SMEM] + [VMEM] * 7,
        out_specs=VMEM,
        compiler_params=pltpu.CompilerParams(vmem_limit_bytes=24 * 2**20),
        name="combine",
    )(info, own, from_sib, across, corner, w_local, w_across, w_corner)


def solution(mesh):
    placed = (
        P("seq", None, "grp"), P(), P(), P(), P("seq", None, "grp"), P(), P("seq", None), P("seq"),
        P(), P(), P(), P(), P(None, "grp"), P(None, "grp"), P(None, "grp"), P(), P(), P("grp", None),
    )
    return jax.shard_map(local, mesh=mesh, in_specs=placed, out_specs=P("seq", "grp"), check_vma=False)
```

```python
import functools
import math

import jax
import jax.numpy as jnp
from jax import lax
from jax.experimental import pallas as pl
from jax.experimental.pallas import tpu as pltpu
from jax.sharding import PartitionSpec as P

STEPS = 50
EPSILON = 1e-06
F32 = jnp.float32
BF16 = jnp.bfloat16
VMEM = pl.BlockSpec(memory_space=pltpu.VMEM)
SMEM = pl.BlockSpec(memory_space=pltpu.SMEM)


def dot(a, b):
    return jnp.dot(a, b, preferred_element_type=F32)


def time_embed(step_index, width):
    half_width = width // 2
    frequency = jnp.exp(-math.log(10000.0) * jnp.arange(half_width, dtype=F32) / half_width)
    angles = (step_index[0].astype(F32) * frequency).reshape(1, half_width)
    return jnp.cos(angles), jnp.sin(angles)


def column_of(row):
    count = row.shape[1]
    diagonal = lax.broadcasted_iota(jnp.int32, (count, count), 0) == lax.broadcasted_iota(
        jnp.int32, (count, count), 1
    )
    return jnp.sum(jnp.where(diagonal, row.astype(F32), 0.0), axis=1, keepdims=True)


def encode_kernel(
    step_ref, feats_ref, earlier_ref, weight_ref, bias_ref, latent_ref, noise_ref, hist_ref,
    level_ref, out_ref,
):
    frames, channels, pixels = feats_ref.shape
    lat = noise_ref.shape[1]
    patch = lat * 4
    cells = pixels // 4
    bias = column_of(bias_ref[...])
    step = jnp.full((lat, pixels), step_ref[0].astype(F32), F32)
    sigma = (STEPS - step) / STEPS
    row = lax.broadcasted_iota(jnp.int32, (lat, frames * patch), 0)
    lane = lax.broadcasted_iota(jnp.int32, (lat, frames * patch), 1)
    pixel = lax.broadcasted_iota(jnp.int32, (pixels, frames * patch), 0)
    feature = lax.broadcasted_iota(jnp.int32, (pixels, frames * patch), 1)
    keep = (pixel % 4) == (feature % 4)
    collect = (
        lax.broadcasted_iota(jnp.int32, (cells, pixels), 1) // 4
        == lax.broadcasted_iota(jnp.int32, (cells, pixels), 0)
    ).astype(BF16)
    patches = jnp.zeros((cells, frames * patch), F32)
    for t in range(frames):
        total = jnp.zeros((channels, pixels), F32)
        for tap in range(3):
            source = t - tap
            window = feats_ref[source] if source >= 0 else earlier_ref[frames + source]
            total = total + dot(weight_ref[tap], window)
        total = total + bias
        hidden = (total / (1.0 + jnp.exp(-total))).astype(BF16)
        mixed = dot(latent_ref[...], hidden)
        noisy = ((1.0 - sigma) * mixed + sigma * noise_ref[t].astype(F32)).astype(BF16)
        spread = (lane // 4 == row + t * lat).astype(BF16)
        wide = lax.dot_general(noisy, spread, (((0,), (0,)), ((), ())), preferred_element_type=F32)
        wide = jnp.where(keep, wide, 0.0).astype(BF16)
        patches = patches + dot(collect, wide)
    out_ref[0:cells, :] = patches.astype(BF16)
    slots = hist_ref.shape[0]
    level = jnp.broadcast_to(column_of(level_ref[...]), (slots, patch))
    tail = jnp.concatenate([hist_ref[...].astype(F32), level], axis=1)
    tail = jnp.concatenate([tail, jnp.zeros((out_ref.shape[0] - cells - slots, 2 * patch), F32)], axis=0)
    out_ref[cells:, :] = tail.astype(BF16)


def exact_parts(values):
    high = values.astype(BF16)
    rest = values - high.astype(F32)
    middle = rest.astype(BF16)
    return high, middle, (rest - middle.astype(F32)).astype(BF16)


def joint_kernel(*refs, cells, block, pieces, owner_masks, tile, query_rows):
    near, far = refs[:pieces], refs[pieces : 2 * pieces]
    (
        count_ref, w_in_ref, w_hist_ref, cos_ref, sin_ref, gain_ref, w_query_ref, w_key_ref, w_value_ref,
        q_gain_ref, k_gain_ref, hist_ref, own_ref, sib_ref,
        patch_ref, wide_ref, w_q_ref, w_kv_ref, tok_a_ref, tok_b_ref, q_ref, k_ref, v_ref, s_a_ref,
        s_b_ref, x_ref, out_ref, semaphores,
    ) = refs[2 * pieces :]
    heads, keys, size = k_ref.shape
    patch, width = w_in_ref.shape
    depth = heads * size
    lanes = near[0].shape[1]
    frames = lanes // patch
    rows = 4 * cells * frames
    group = lax.axis_index("grp")
    place = lax.axis_index("seq")
    start = pl.multiple_of((place % 2) * depth, depth)
    copies = [
        pltpu.make_async_copy(w_query_ref.at[:, pl.ds(start, depth)], w_q_ref, semaphores.at[0]),
        pltpu.make_async_copy(
            w_key_ref.at[:, pl.ds(start, depth)], w_kv_ref.at[:, 0:depth], semaphores.at[1]
        ),
        pltpu.make_async_copy(
            w_value_ref.at[:, pl.ds(start, depth)], w_kv_ref.at[:, depth : 2 * depth], semaphores.at[2]
        ),
    ]
    for copy in copies:
        copy.start()

    step = 512
    lane = lax.broadcasted_iota(jnp.int32, (1, lanes), 1)
    for n, source in ((0, cos_ref), (width // 2, sin_ref)):
        values = source[...]
        row = lax.broadcasted_iota(jnp.int32, (lanes - patch, values.shape[1]), 0)
        high, middle, low = exact_parts(values)
        extra = jnp.where(row == 0, high.astype(F32), 0.0)
        extra = jnp.where(row == 1, middle.astype(F32), extra)
        extra = jnp.where(row == 2, low.astype(F32), extra)
        wide_ref[patch:lanes, n : n + values.shape[1]] = extra.astype(BF16)
    wide_ref[0:patch, :] = w_in_ref[...]
    gram = jnp.zeros((lanes, lanes), F32)
    for n in range(0, width, step):
        part = wide_ref[:, n : n + step]
        gram = gram + lax.dot_general(part, part, (((1,), (1,)), ((), ())), preferred_element_type=F32)
    gram_parts = jnp.concatenate(exact_parts(gram), axis=0)

    ones = jnp.where(lane < patch + 3, 1.0, 0.0)
    held = near[0].shape[0] // block
    half = pieces * held
    fours = []
    for sources in (near, far):
        mine = sources[0][0:cells, :]
        theirs = sources[pieces // 2][0:cells, :]
        fours.append(jnp.where(group == 0, mine, theirs))
        fours.append(jnp.where(group == 0, theirs, mine))
    for sources in (near, far):
        for p in range(half):
            if p != 0 and p != half // 2:
                fours.append((sources[p // held], (p % held) * block))
    for spot, item in enumerate(fours):
        values = (item[0][item[1] : item[1] + cells, :] if isinstance(item, tuple) else item).astype(F32)
        for t in range(frames):
            moved = values if t == 0 else pltpu.roll(values, lanes - t * patch, 1)
            at = (spot // 4) * rows + t * 4 * cells + (spot % 4) * cells
            patch_ref[at : at + cells, :] = jnp.where(lane < patch, moved, ones).astype(BF16)

    def tokens_of(i, tok_ref):
        source = patch_ref[pl.ds(pl.multiple_of(i * tile, tile), tile), :]
        mixed = dot(jnp.concatenate([source] * 3, axis=1), gram_parts)
        mean = jnp.sum(mixed * source.astype(F32), axis=1, keepdims=True) / width
        inverse = lax.rsqrt(mean + EPSILON)
        for n in range(0, width, step):
            x = dot(source, wide_ref[:, n : n + step])
            tok_ref[:, n : n + step] = (x * inverse * gain_ref[:, n : n + step]).astype(BF16)

    def head_norm(values, gain):
        mean = jnp.mean(values * values, axis=1, keepdims=True)
        return (values * lax.rsqrt(mean + EPSILON) * gain).astype(BF16)

    def project(tokens, at):
        both = dot(tokens, w_kv_ref[...])
        count = tokens.shape[0]
        for h in range(heads):
            k_ref[h, pl.ds(at, count), :] = head_norm(both[:, h * size : (h + 1) * size], k_gain_ref[...])
            v_ref[h, pl.ds(at, count), :] = both[:, (heads + h) * size : (heads + h + 1) * size].astype(BF16)

    tokens_of(0, tok_a_ref)
    copies[0].wait()
    q = dot(tok_a_ref[0:rows, :], w_q_ref[...])
    for h in range(heads):
        q_ref[h] = head_norm(q[:, h * size : (h + 1) * size], q_gain_ref[...])
    copies[1].wait()
    copies[2].wait()
    tiles = patch_ref.shape[0] // tile

    def pair(j, carry):
        tokens_of(2 * j + 1, tok_b_ref)
        project(tok_a_ref[...], pl.multiple_of(2 * j * tile, tile))
        tokens_of(2 * j + 2, tok_a_ref)
        project(tok_b_ref[...], pl.multiple_of((2 * j + 1) * tile, tile))
        return carry

    if tiles > 2:
        lax.fori_loop(0, tiles // 2 - 1, pair, 0)
    tokens_of(tiles - 1, tok_b_ref)
    project(tok_a_ref[...], (tiles - 2) * tile)
    project(tok_b_ref[...], (tiles - 1) * tile)

    section = tiles * tile
    slots = hist_ref.shape[0]
    levels = w_hist_ref.shape[0]
    owners = len(owner_masks)
    spread = 128 // slots
    owner_blocks = [
        (sources[p // held], (p % held) * block + cells) for sources in (near, far) for p in range(half // 2)
    ]
    biases = []
    for r in range(0, owners, spread):
        taken = owner_blocks[r : r + spread]
        source = jnp.concatenate([ref[at : at + 16, :].astype(F32)[0:slots] for ref, at in taken], axis=0)
        count = source.shape[0]
        values, level = source[:, 0:patch], source[:, patch : 2 * patch]
        parts = [jnp.where(level == v, values, 0.0).astype(BF16) for v in range(levels)]
        squares = jnp.zeros((count, 128), F32)
        for n in range(0, width, step):
            x = dot(parts[0], w_hist_ref[0, :, n : n + step])
            for v in range(1, levels):
                x = x + dot(parts[v], w_hist_ref[v, :, n : n + step])
            x_ref[0:count, n : n + step] = x
            for m in range(0, step, 128):
                squares = squares + x[:, m : m + 128] * x[:, m : m + 128]
        inverse = lax.rsqrt(jnp.sum(squares, axis=1, keepdims=True) / width + EPSILON)
        for n in range(0, width, step):
            tok_a_ref[0:count, n : n + step] = (
                x_ref[0:count, n : n + step] * inverse * gain_ref[:, n : n + step]
            ).astype(BF16)
        project(tok_a_ref[0:count, :], section + r * slots)
        slot = lax.broadcasted_iota(jnp.int32, (1, count), 1)
        live = jnp.zeros((1, count), jnp.int32)
        for o in range(len(taken)):
            live = jnp.where(slot // slots == o, count_ref[place ^ owner_masks[r + o]], live)
        biases.append(jnp.where(slot % slots < live, 0.0, -1e30))

    scale = math.log2(math.e) / math.sqrt(size)
    chunk = 512
    fold = 128
    parts = [(a, chunk, None) for a in range(0, section, chunk)]
    parts += [(section + r * spread * slots, b.shape[1], b) for r, b in enumerate(biases)]
    units = [(h, a) for h in range(heads) for a in range(0, rows, query_rows)]
    buffers = (s_a_ref, s_b_ref)

    def score(unit, state, part):
        h, a = units[unit]
        at, length, bias = part
        for n in range(at, at + length, 256):
            span = min(256, at + length - n)
            s = lax.dot_general(
                q_ref[h, a : a + query_rows, :], k_ref[h, n : n + span, :], (((1,), (1,)), ((), ())),
                preferred_element_type=F32,
            )
            if bias is not None:
                s = s + bias[:, n - at : n - at + span]
            buffers[unit % 2][:, n : n + span] = s
            for m in range(0, span, fold):
                state = jnp.maximum(state, s[:, m : m + fold])
        return state

    fresh = jnp.full((query_rows, fold), -3e38, F32)
    state = fresh
    for part in parts:
        state = score(0, state, part)
    for unit, (h, a) in enumerate(units):
        top = jnp.max(state, axis=1, keepdims=True)
        state = fresh
        total = jnp.zeros((query_rows, fold), F32)
        weighted = jnp.zeros((query_rows, size), F32)
        for part in parts:
            at, length, _ = part
            soft = jnp.exp2((buffers[unit % 2][:, at : at + length] - top) * scale)
            for m in range(0, length, fold):
                total = total + soft[:, m : m + fold]
            weighted = weighted + dot(soft.astype(BF16), v_ref[h, at : at + length, :])
            if unit + 1 < len(units):
                state = score(unit + 1, state, part)
        out_ref[a : a + query_rows, h * size : (h + 1) * size] = (
            weighted / jnp.sum(total, axis=1, keepdims=True)
        ).astype(BF16)
    part = 2 * cells
    for t in range(frames):
        base = t * 4 * cells
        own_ref[t * part : (t + 1) * part, :] = out_ref[base : base + part, :]
        sib_ref[t * part : (t + 1) * part, :] = out_ref[base + part : base + 2 * part, :]


def combine_kernel(
    own_ref, sib_ref, across_ref, corner_ref, w_local_ref, w_across_ref, w_corner_ref, out_ref
):
    core = lax.axis_index("seq") % 2
    depth = own_ref.shape[1]
    mine = pl.ds(pl.multiple_of(core * depth, depth), depth)
    other = pl.ds(pl.multiple_of((1 - core) * depth, depth), depth)
    step = 512
    for n in range(0, out_ref.shape[1], step):
        columns = slice(n, n + step)
        total = dot(own_ref[...], w_local_ref[mine, columns])
        total = total + dot(sib_ref[...], w_local_ref[other, columns])
        total = total + dot(across_ref[...], w_across_ref[:, columns])
        total = total + dot(corner_ref[...], w_corner_ref[:, columns])
        out_ref[:, columns] = total.astype(BF16)


def flip(value, mask, seq_count):
    pairs = [(i, i ^ mask) for i in range(2 * seq_count)]
    return lax.ppermute(value, ("grp", "seq"), pairs)


def local(
    feats, conv_weight, conv_bias, latent_projection_weight, noise, step_index, hist, hist_level,
    hist_count, w_in, w_hist, norm_gain, w_query, w_key, w_value, q_gain, k_gain, w_out,
):
    frame_count, channels, pixels = feats.shape
    seq_count = lax.axis_size("seq")
    group = lax.axis_index("grp")
    place = lax.axis_index("seq")
    core = place % 2
    width = w_in.shape[1]
    patch = w_in.shape[0]
    cells = pixels // 4
    slots = hist.shape[0]
    block = cells + 16
    lanes = frame_count * patch
    size = q_gain.shape[0]
    heads = w_query.shape[1] // size // 2
    depth = heads * size

    earlier = lax.ppermute(feats, "seq", [(i, i + 1) for i in range(seq_count - 1)])
    gathered = pl.pallas_call(
        encode_kernel,
        out_shape=jax.ShapeDtypeStruct((block, lanes), BF16),
        in_specs=[SMEM] + [VMEM] * 8,
        out_specs=VMEM,
        name="encode",
    )(
        step_index, feats, earlier, conv_weight, conv_bias.reshape(1, channels),
        latent_projection_weight, noise, hist, hist_level.reshape(1, slots),
    )

    bits = []
    bit = seq_count // 2
    while bit > 1:
        bits.append(bit)
        bit //= 2
    owner_masks = [0]
    for bit in bits:
        owner_masks = owner_masks + [m ^ bit for m in owner_masks]
    owner_masks = tuple(owner_masks + [m ^ 1 for m in owner_masks])
    bits.append(seq_count)
    rounds = [bits[i : i + 2] for i in range(len(bits) % 2, len(bits), 2)]
    if len(bits) % 2:
        rounds = [bits[:1]] + rounds
    for number, pair in enumerate(rounds):
        masks = [0] + [pair[0]] + ([pair[1], pair[0] ^ pair[1]] if len(pair) > 1 else [])
        near = [gathered] + [flip(gathered, mask, seq_count) for mask in masks[1:]]
        if number + 1 < len(rounds):
            gathered = jnp.concatenate(near, axis=0)
    far = [flip(piece, 1, seq_count) for piece in near]

    columns = w_out.shape[1] // 2
    w_send = lax.dynamic_slice(w_out, (core * depth, (1 - group) * columns), (depth, columns))
    w_send, *near = lax.optimization_barrier((w_send, *near))
    w_across = flip(w_send, seq_count, seq_count)
    w_local = lax.dynamic_slice_in_dim(w_out, group * columns, columns, axis=1)

    tokens = 2 * seq_count * frame_count * cells
    keys = tokens + slots * seq_count
    rows = frame_count * 4 * cells
    tile = 2 * rows
    query_rows = rows
    while 2 * query_rows * keys * 4 > 12 * 2**20:
        query_rows //= 2
    cos, sin = time_embed(step_index, width)
    anywhere = pl.BlockSpec(memory_space=pl.ANY)
    own, sib = pl.pallas_call(
        functools.partial(
            joint_kernel, cells=cells, block=block, pieces=len(near), owner_masks=owner_masks, tile=tile,
            query_rows=query_rows,
        ),
        out_shape=[jax.ShapeDtypeStruct((rows // 2, depth), BF16)] * 2,
        in_specs=[VMEM] * (2 * len(near)) + [SMEM] + [VMEM] * 5 + [anywhere] * 3 + [VMEM] * 3,
        out_specs=[VMEM] * 2,
        scratch_shapes=[
            pltpu.VMEM((tokens, lanes), BF16),
            pltpu.VMEM((lanes, width), BF16),
            pltpu.VMEM((width, depth), BF16),
            pltpu.VMEM((width, 2 * depth), BF16),
            pltpu.VMEM((tile, width), BF16),
            pltpu.VMEM((tile, width), BF16),
            pltpu.VMEM((heads, rows, size), BF16),
            pltpu.VMEM((heads, keys, size), BF16),
            pltpu.VMEM((heads, keys, size), BF16),
            pltpu.VMEM((query_rows, keys), F32),
            pltpu.VMEM((query_rows, keys), F32),
            pltpu.VMEM((128, width), F32),
            pltpu.VMEM((rows, depth), BF16),
            pltpu.SemaphoreType.DMA((3,)),
        ],
        compiler_params=pltpu.CompilerParams(vmem_limit_bytes=60 * 2**20),
        cost_estimate=pl.CostEstimate(
            flops=2 * keys * width * 3 * depth + 4 * rows * keys * depth,
            bytes_accessed=6 * width * depth,
            transcendentals=rows * keys * heads,
        ),
        name="joint",
    )(
        *near, *far, hist_count, w_in, w_hist, cos, sin, norm_gain.reshape(1, width), w_query, w_key,
        w_value, q_gain.reshape(1, size), k_gain.reshape(1, size), hist,
    )
    w_across, own, sib = lax.optimization_barrier((w_across, own, sib))
    w_corner = flip(w_across, 1, seq_count)
    from_sib = flip(sib, 1, seq_count)
    across = flip(own, seq_count, seq_count)
    corner = flip(sib, seq_count + 1, seq_count)
    return pl.pallas_call(
        combine_kernel,
        out_shape=jax.ShapeDtypeStruct((rows // 2, columns), BF16),
        in_specs=[VMEM] * 7,
        out_specs=VMEM,
        compiler_params=pltpu.CompilerParams(vmem_limit_bytes=24 * 2**20),
        name="combine",
    )(own, from_sib, across, corner, w_local, w_across, w_corner)


def solution(mesh):
    placed = (
        P("seq", None, "grp"), P(), P(), P(), P("seq", None, "grp"), P(), P("seq", None), P("seq"),
        P(), P(), P(), P(), P(None, "grp"), P(None, "grp"), P(None, "grp"), P(), P(), P("grp", None),
    )
    return jax.shard_map(local, mesh=mesh, in_specs=placed, out_specs=P("seq", "grp"), check_vma=False)
```

```python
import functools
import math

import jax
import jax.numpy as jnp
from jax import lax
from jax.experimental import pallas as pl
from jax.experimental.pallas import tpu as pltpu
from jax.sharding import PartitionSpec as P

STEPS = 50
EPSILON = 1e-06
F32 = jnp.float32
BF16 = jnp.bfloat16
VMEM = pl.BlockSpec(memory_space=pltpu.VMEM)
SMEM = pl.BlockSpec(memory_space=pltpu.SMEM)


def dot(a, b):
    return jnp.dot(a, b, preferred_element_type=F32)


def dot_rows(a, b):
    return lax.dot_general(a, b, (((1,), (1,)), ((), ())), preferred_element_type=F32)


def time_embed(step_index, width):
    half_width = width // 2
    frequency = jnp.exp(-math.log(10000.0) * jnp.arange(half_width, dtype=F32) / half_width)
    angles = (step_index[0].astype(F32) * frequency).reshape(1, half_width)
    return jnp.cos(angles), jnp.sin(angles)


def column_of(row):
    count = row.shape[1]
    diagonal = lax.broadcasted_iota(jnp.int32, (count, count), 0) == lax.broadcasted_iota(
        jnp.int32, (count, count), 1
    )
    return jnp.sum(jnp.where(diagonal, row.astype(F32), 0.0), axis=1, keepdims=True)


def encode_kernel(step_ref, earlier_ref, partial_ref, weight_ref, latent_ref, noise_ref, tail_ref, out_ref):
    frames, pixels, channels = partial_ref.shape
    lat = noise_ref.shape[1]
    patch = lat * 4
    cells = pixels // 4
    taps = weight_ref.shape[0] + 1
    step = jnp.full((lat, pixels), step_ref[0].astype(F32), F32)
    sigma = (STEPS - step) / STEPS
    row = lax.broadcasted_iota(jnp.int32, (lat, frames * patch), 0)
    lane = lax.broadcasted_iota(jnp.int32, (lat, frames * patch), 1)
    pixel = lax.broadcasted_iota(jnp.int32, (pixels, frames * patch), 0)
    feature = lax.broadcasted_iota(jnp.int32, (pixels, frames * patch), 1)
    keep = (pixel % 4) == (feature % 4)
    collect = (
        lax.broadcasted_iota(jnp.int32, (cells, pixels), 1) // 4
        == lax.broadcasted_iota(jnp.int32, (cells, pixels), 0)
    ).astype(BF16)
    patches = jnp.zeros((cells, frames * patch), F32)
    for t in range(frames):
        total = partial_ref[t]
        for tap in range(t + 1, taps):
            total = total + dot_rows(earlier_ref[frames + t - tap], weight_ref[tap - 1])
        hidden = (total / (1.0 + jnp.exp(-total))).astype(BF16)
        mixed = dot_rows(latent_ref[...], hidden)
        noisy = ((1.0 - sigma) * mixed + sigma * noise_ref[t].astype(F32)).astype(BF16)
        spread = (lane // 4 == row + t * lat).astype(BF16)
        wide = lax.dot_general(noisy, spread, (((0,), (0,)), ((), ())), preferred_element_type=F32)
        wide = jnp.where(keep, wide, 0.0).astype(BF16)
        patches = patches + dot(collect, wide)
    out_ref[0:cells, :] = patches.astype(BF16)
    out_ref[cells:, :] = tail_ref[...]


def exact_parts(values):
    high = values.astype(BF16)
    rest = values - high.astype(F32)
    middle = rest.astype(BF16)
    return high, middle, (rest - middle.astype(F32)).astype(BF16)


def prepare_kernel(
    w_in_ref, cos_ref, sin_ref, feats_ref, weight_ref, bias_ref, latent_ref, noise_ref, hist_ref, level_ref,
    wide_ref, gram_ref, partial_ref, taps_ref, latent_out_ref, noise_out_ref, tail_ref,
):
    frames, pixels, channels = feats_ref.shape
    for t in range(frames):
        total = jnp.broadcast_to(bias_ref[...], (pixels, channels))
        for tap in range(t + 1):
            total = total + dot_rows(feats_ref[t - tap], weight_ref[tap])
        partial_ref[t] = total
    taps_ref[...] = weight_ref[1:]
    latent_out_ref[...] = latent_ref[...]
    noise_out_ref[...] = noise_ref[...]
    patch, width = w_in_ref.shape
    slots = hist_ref.shape[0]
    level = jnp.broadcast_to(column_of(level_ref[...]), (slots, patch))
    tail = jnp.concatenate([hist_ref[...].astype(F32), level], axis=1)
    rest = jnp.zeros((tail_ref.shape[0] - slots, 2 * patch), F32)
    tail_ref[...] = jnp.concatenate([tail, rest], axis=0).astype(BF16)
    lanes = wide_ref.shape[0]
    for n, source in ((0, cos_ref), (width // 2, sin_ref)):
        values = source[...]
        row = lax.broadcasted_iota(jnp.int32, (lanes - patch, values.shape[1]), 0)
        high, middle, low = exact_parts(values)
        extra = jnp.where(row == 0, high.astype(F32), 0.0)
        extra = jnp.where(row == 1, middle.astype(F32), extra)
        extra = jnp.where(row == 2, low.astype(F32), extra)
        wide_ref[patch:lanes, n : n + values.shape[1]] = extra.astype(BF16)
    wide_ref[0:patch, :] = w_in_ref[...]
    gram = jnp.zeros((lanes, lanes), F32)
    step = 512
    for n in range(0, width, step):
        part = wide_ref[:, n : n + step]
        gram = gram + dot_rows(part, part)
    for number, part in enumerate(exact_parts(gram)):
        gram_ref[number * lanes : (number + 1) * lanes, :] = part


def joint_kernel(*refs, cells, block, pieces, owner_masks, tile, query_rows):
    near, far = refs[:pieces], refs[pieces : 2 * pieces]
    (
        count_ref, wide_ref, gram_ref, w_hist_ref, gain_ref, w_query_ref, w_key_ref, w_value_ref,
        q_gain_ref, k_gain_ref, hist_ref, own_ref, sib_ref,
        patch_ref, w_q_ref, w_kv_ref, tok_a_ref, tok_b_ref, q_ref, k_ref, v_ref, s_a_ref,
        s_b_ref, x_ref, out_ref, semaphores,
    ) = refs[2 * pieces :]
    heads, keys, size = k_ref.shape
    levels, patch, width = w_hist_ref.shape
    depth = heads * size
    lanes = near[0].shape[1]
    frames = lanes // patch
    rows = 4 * cells * frames
    group = lax.axis_index("grp")
    place = lax.axis_index("seq")
    start = pl.multiple_of((place % 2) * depth, depth)
    copies = [
        pltpu.make_async_copy(w_query_ref.at[:, pl.ds(start, depth)], w_q_ref, semaphores.at[0]),
        pltpu.make_async_copy(
            w_key_ref.at[:, pl.ds(start, depth)], w_kv_ref.at[:, 0:depth], semaphores.at[1]
        ),
        pltpu.make_async_copy(
            w_value_ref.at[:, pl.ds(start, depth)], w_kv_ref.at[:, depth : 2 * depth], semaphores.at[2]
        ),
    ]
    for copy in copies:
        copy.start()

    step = 512
    lane = lax.broadcasted_iota(jnp.int32, (1, lanes), 1)
    ones = jnp.where(lane < patch + 3, 1.0, 0.0)
    held = near[0].shape[0] // block
    half = pieces * held
    fours = []
    for sources in (near, far):
        mine = sources[0][0:cells, :]
        theirs = sources[pieces // 2][0:cells, :]
        fours.append(jnp.where(group == 0, mine, theirs))
        fours.append(jnp.where(group == 0, theirs, mine))
    for sources in (near, far):
        for p in range(half):
            if p != 0 and p != half // 2:
                fours.append((sources[p // held], (p % held) * block))
    for spot, item in enumerate(fours):
        values = (item[0][item[1] : item[1] + cells, :] if isinstance(item, tuple) else item).astype(F32)
        for t in range(frames):
            moved = values if t == 0 else pltpu.roll(values, lanes - t * patch, 1)
            at = (spot // 4) * rows + t * 4 * cells + (spot % 4) * cells
            patch_ref[at : at + cells, :] = jnp.where(lane < patch, moved, ones).astype(BF16)

    def tokens_of(i, tok_ref):
        source = patch_ref[pl.ds(pl.multiple_of(i * tile, tile), tile), :]
        mixed = dot(jnp.concatenate([source] * 3, axis=1), gram_ref[...])
        mean = jnp.sum(mixed * source.astype(F32), axis=1, keepdims=True) / width
        inverse = lax.rsqrt(mean + EPSILON)
        for n in range(0, width, step):
            x = dot(source, wide_ref[:, n : n + step])
            tok_ref[:, n : n + step] = (x * inverse * gain_ref[:, n : n + step]).astype(BF16)

    def head_norm(values, gain):
        mean = jnp.mean(values * values, axis=1, keepdims=True)
        return (values * lax.rsqrt(mean + EPSILON) * gain).astype(BF16)

    def project(tokens, at):
        both = dot(tokens, w_kv_ref[...])
        count = tokens.shape[0]
        for h in range(heads):
            k_ref[h, pl.ds(at, count), :] = head_norm(both[:, h * size : (h + 1) * size], k_gain_ref[...])
            v_ref[h, pl.ds(at, count), :] = both[:, (heads + h) * size : (heads + h + 1) * size].astype(BF16)

    tokens_of(0, tok_a_ref)
    for copy in copies:
        copy.wait()
    q = dot(tok_a_ref[0:rows, :], w_q_ref[...])
    for h in range(heads):
        q_ref[h] = head_norm(q[:, h * size : (h + 1) * size], q_gain_ref[...])
    tiles = patch_ref.shape[0] // tile

    def pair(j, carry):
        tokens_of(2 * j + 1, tok_b_ref)
        project(tok_a_ref[...], pl.multiple_of(2 * j * tile, tile))
        tokens_of(2 * j + 2, tok_a_ref)
        project(tok_b_ref[...], pl.multiple_of((2 * j + 1) * tile, tile))
        return carry

    if tiles > 2:
        lax.fori_loop(0, tiles // 2 - 1, pair, 0)
    tokens_of(tiles - 1, tok_b_ref)
    project(tok_a_ref[...], (tiles - 2) * tile)
    project(tok_b_ref[...], (tiles - 1) * tile)

    section = tiles * tile
    slots = hist_ref.shape[0]
    owners = len(owner_masks)
    spread = 128 // slots
    owner_blocks = [
        (sources[p // held], (p % held) * block + cells) for sources in (near, far) for p in range(half // 2)
    ]
    biases = []
    for r in range(0, owners, spread):
        taken = owner_blocks[r : r + spread]
        source = jnp.concatenate([ref[at : at + 16, :].astype(F32)[0:slots] for ref, at in taken], axis=0)
        count = source.shape[0]
        values, level = source[:, 0:patch], source[:, patch : 2 * patch]
        parts = [jnp.where(level == v, values, 0.0).astype(BF16) for v in range(levels)]
        squares = jnp.zeros((count, 128), F32)
        for n in range(0, width, step):
            x = dot(parts[0], w_hist_ref[0, :, n : n + step])
            for v in range(1, levels):
                x = x + dot(parts[v], w_hist_ref[v, :, n : n + step])
            x_ref[0:count, n : n + step] = x
            for m in range(0, step, 128):
                squares = squares + x[:, m : m + 128] * x[:, m : m + 128]
        inverse = lax.rsqrt(jnp.sum(squares, axis=1, keepdims=True) / width + EPSILON)
        for n in range(0, width, step):
            tok_a_ref[0:count, n : n + step] = (
                x_ref[0:count, n : n + step] * inverse * gain_ref[:, n : n + step]
            ).astype(BF16)
        project(tok_a_ref[0:count, :], section + r * slots)
        slot = lax.broadcasted_iota(jnp.int32, (1, count), 1)
        live = jnp.zeros((1, count), jnp.int32)
        for o in range(len(taken)):
            live = jnp.where(slot // slots == o, count_ref[place ^ owner_masks[r + o]], live)
        biases.append(jnp.where(slot % slots < live, 0.0, -1e30))

    scale = math.log2(math.e) / math.sqrt(size)
    chunk = 512
    fold = 128
    parts = [(a, chunk, None) for a in range(0, section, chunk)]
    parts += [(section + r * spread * slots, b.shape[1], b) for r, b in enumerate(biases)]
    units = [(h, a) for h in range(heads) for a in range(0, rows, query_rows)]
    buffers = (s_a_ref, s_b_ref)

    def score(unit, state, part):
        h, a = units[unit]
        at, length, bias = part
        for n in range(at, at + length, 256):
            span = min(256, at + length - n)
            s = lax.dot_general(
                q_ref[h, a : a + query_rows, :], k_ref[h, n : n + span, :], (((1,), (1,)), ((), ())),
                preferred_element_type=F32,
            )
            if bias is not None:
                s = s + bias[:, n - at : n - at + span]
            buffers[unit % 2][:, n : n + span] = s
            for m in range(0, span, fold):
                state = jnp.maximum(state, s[:, m : m + fold])
        return state

    fresh = jnp.full((query_rows, fold), -3e38, F32)
    state = fresh
    for part in parts:
        state = score(0, state, part)
    for unit, (h, a) in enumerate(units):
        top = jnp.max(state, axis=1, keepdims=True)
        state = fresh
        total = jnp.zeros((query_rows, fold), F32)
        weighted = jnp.zeros((query_rows, size), F32)
        for part in parts:
            at, length, _ = part
            soft = jnp.exp2((buffers[unit % 2][:, at : at + length] - top) * scale)
            for m in range(0, length, fold):
                total = total + soft[:, m : m + fold]
            weighted = weighted + dot(soft.astype(BF16), v_ref[h, at : at + length, :])
            if unit + 1 < len(units):
                state = score(unit + 1, state, part)
        out_ref[a : a + query_rows, h * size : (h + 1) * size] = (
            weighted / jnp.sum(total, axis=1, keepdims=True)
        ).astype(BF16)
    part = 2 * cells
    for t in range(frames):
        base = t * 4 * cells
        own_ref[t * part : (t + 1) * part, :] = out_ref[base : base + part, :]
        sib_ref[t * part : (t + 1) * part, :] = out_ref[base + part : base + 2 * part, :]


def combine_kernel(
    own_ref, sib_ref, across_ref, corner_ref, w_local_ref, w_across_ref, w_corner_ref, out_ref
):
    core = lax.axis_index("seq") % 2
    depth = own_ref.shape[1]
    mine = pl.ds(pl.multiple_of(core * depth, depth), depth)
    other = pl.ds(pl.multiple_of((1 - core) * depth, depth), depth)
    step = 512
    for n in range(0, out_ref.shape[1], step):
        columns = slice(n, n + step)
        total = dot(own_ref[...], w_local_ref[mine, columns])
        total = total + dot(sib_ref[...], w_local_ref[other, columns])
        total = total + dot(across_ref[...], w_across_ref[:, columns])
        total = total + dot(corner_ref[...], w_corner_ref[:, columns])
        out_ref[:, columns] = total.astype(BF16)


def in_hbm(*values):
    return [pltpu.with_memory_space_constraint(value, pltpu.HBM) for value in values]


def flip(value, mask, seq_count):
    pairs = [(i, i ^ mask) for i in range(2 * seq_count)]
    return lax.ppermute(value, ("grp", "seq"), pairs)


def local(
    feats, conv_weight, conv_bias, latent_projection_weight, noise, step_index, hist, hist_level,
    hist_count, w_in, w_hist, norm_gain, w_query, w_key, w_value, q_gain, k_gain, w_out,
):
    frame_count, channels, pixels = feats.shape
    seq_count = lax.axis_size("seq")
    group = lax.axis_index("grp")
    place = lax.axis_index("seq")
    core = place % 2
    width = w_in.shape[1]
    patch = w_in.shape[0]
    cells = pixels // 4
    slots = hist.shape[0]
    block = cells + 16
    lanes = frame_count * patch
    size = q_gain.shape[0]
    heads = w_query.shape[1] // size // 2
    depth = heads * size

    swapped = feats.transpose(0, 2, 1)
    earlier = lax.ppermute(swapped, "seq", [(i, i + 1) for i in range(seq_count - 1)])
    cos, sin = time_embed(step_index, width)
    wide, gram, partial, taps, latent, held_noise, tail = pl.pallas_call(
        prepare_kernel,
        out_shape=[
            jax.ShapeDtypeStruct((lanes, width), BF16),
            jax.ShapeDtypeStruct((3 * lanes, lanes), BF16),
            jax.ShapeDtypeStruct(swapped.shape, F32),
            jax.ShapeDtypeStruct((conv_weight.shape[0] - 1,) + conv_weight.shape[1:], BF16),
            jax.ShapeDtypeStruct(latent_projection_weight.shape, BF16),
            jax.ShapeDtypeStruct(noise.shape, BF16),
            jax.ShapeDtypeStruct((block - cells, lanes), BF16),
        ],
        in_specs=[VMEM] * 10,
        out_specs=[VMEM] * 7,
        compiler_params=pltpu.CompilerParams(vmem_limit_bytes=10 * 2**20),
        name="prepare",
    )(
        *in_hbm(
            w_in, cos, sin, swapped, conv_weight, conv_bias.reshape(1, channels),
            latent_projection_weight, noise, hist, hist_level.reshape(1, slots),
        )
    )
    earlier, partial = lax.optimization_barrier((earlier, partial))
    gathered = pl.pallas_call(
        encode_kernel,
        out_shape=jax.ShapeDtypeStruct((block, lanes), BF16),
        in_specs=[SMEM] + [VMEM] * 6,
        out_specs=VMEM,
        compiler_params=pltpu.CompilerParams(vmem_limit_bytes=6 * 2**20),
        name="encode",
    )(step_index, earlier, partial, taps, latent, held_noise, tail)
    columns = w_out.shape[1] // 2
    w_send = lax.dynamic_slice(w_out, (core * depth, (1 - group) * columns), (depth, columns))

    bits = []
    bit = seq_count // 2
    while bit > 1:
        bits.append(bit)
        bit //= 2
    owner_masks = [0]
    for bit in bits:
        owner_masks = owner_masks + [m ^ bit for m in owner_masks]
    owner_masks = tuple(owner_masks + [m ^ 1 for m in owner_masks])
    bits.append(seq_count)
    rounds = [bits[i : i + 2] for i in range(len(bits) % 2, len(bits), 2)]
    if len(bits) % 2:
        rounds = [bits[:1]] + rounds
    for number, pair in enumerate(rounds):
        masks = [0] + [pair[0]] + ([pair[1], pair[0] ^ pair[1]] if len(pair) > 1 else [])
        near = [gathered] + [flip(gathered, mask, seq_count) for mask in masks[1:]]
        if number + 1 < len(rounds):
            gathered = jnp.concatenate(near, axis=0)
            gathered, w_send = lax.optimization_barrier((gathered, w_send))
    far = [flip(piece, 1, seq_count) for piece in near]

    w_send, *near = lax.optimization_barrier((w_send, *near))
    w_across = flip(w_send, seq_count, seq_count)
    w_local = lax.dynamic_slice_in_dim(w_out, group * columns, columns, axis=1)

    tokens = 2 * seq_count * frame_count * cells
    keys = tokens + slots * seq_count
    rows = frame_count * 4 * cells
    tile = 2 * rows
    query_rows = rows
    while 2 * query_rows * keys * 4 > 12 * 2**20:
        query_rows //= 2
    limit = (
        2 * tokens * lanes + 6 * width * depth + 4 * tile * width + 4 * keys * depth
        + 8 * query_rows * keys + 512 * width + 4 * rows * depth + 12 * 2**20
    )
    anywhere = pl.BlockSpec(memory_space=pltpu.HBM)
    own, sib = pl.pallas_call(
        functools.partial(
            joint_kernel, cells=cells, block=block, pieces=len(near), owner_masks=owner_masks, tile=tile,
            query_rows=query_rows,
        ),
        out_shape=[jax.ShapeDtypeStruct((rows // 2, depth), BF16)] * 2,
        in_specs=[VMEM] * (2 * len(near)) + [SMEM] + [VMEM] * 4 + [anywhere] * 3 + [VMEM] * 3,
        out_specs=[VMEM] * 2,
        scratch_shapes=[
            pltpu.VMEM((tokens, lanes), BF16),
            pltpu.VMEM((width, depth), BF16),
            pltpu.VMEM((width, 2 * depth), BF16),
            pltpu.VMEM((tile, width), BF16),
            pltpu.VMEM((tile, width), BF16),
            pltpu.VMEM((heads, rows, size), BF16),
            pltpu.VMEM((heads, keys, size), BF16),
            pltpu.VMEM((heads, keys, size), BF16),
            pltpu.VMEM((query_rows, keys), F32),
            pltpu.VMEM((query_rows, keys), F32),
            pltpu.VMEM((128, width), F32),
            pltpu.VMEM((rows, depth), BF16),
            pltpu.SemaphoreType.DMA((3,)),
        ],
        compiler_params=pltpu.CompilerParams(vmem_limit_bytes=limit),
        cost_estimate=pl.CostEstimate(
            flops=2 * keys * width * 3 * depth + 4 * rows * keys * depth,
            bytes_accessed=6 * width * depth,
            transcendentals=rows * keys * heads,
        ),
        name="joint",
    )(
        *near, *far, hist_count, wide, gram, w_hist, norm_gain.reshape(1, width),
        *in_hbm(w_query, w_key, w_value), q_gain.reshape(1, size), k_gain.reshape(1, size), hist,
    )
    w_across, own, sib = lax.optimization_barrier((w_across, own, sib))
    w_corner = flip(w_across, 1, seq_count)
    from_sib = flip(sib, 1, seq_count)
    across = flip(own, seq_count, seq_count)
    corner = flip(sib, seq_count + 1, seq_count)
    return pl.pallas_call(
        combine_kernel,
        out_shape=jax.ShapeDtypeStruct((rows // 2, columns), BF16),
        in_specs=[VMEM] * 7,
        out_specs=VMEM,
        compiler_params=pltpu.CompilerParams(vmem_limit_bytes=10 * 2**20),
        name="combine",
    )(own, from_sib, across, corner, w_local, w_across, w_corner)


def solution(mesh):
    placed = (
        P("seq", None, "grp"), P(), P(), P(), P("seq", None, "grp"), P(), P("seq", None), P("seq"),
        P(), P(), P(), P(), P(None, "grp"), P(None, "grp"), P(None, "grp"), P(), P(), P("grp", None),
    )
    return jax.shard_map(local, mesh=mesh, in_specs=placed, out_specs=P("seq", "grp"), check_vma=False)
```

```python
import functools
import math

import jax
import jax.numpy as jnp
from jax import lax
from jax.experimental import pallas as pl
from jax.experimental.pallas import tpu as pltpu
from jax.sharding import PartitionSpec as P


STEPS = 50
EPSILON = 1e-06
F32 = jnp.float32
BF16 = jnp.bfloat16
VMEM = pl.BlockSpec(memory_space=pltpu.VMEM)
SMEM = pl.BlockSpec(memory_space=pltpu.SMEM)


def dot(a, b):
    return jnp.dot(a, b, preferred_element_type=F32)


def dot_rows(a, b):
    return lax.dot_general(a, b, (((1,), (1,)), ((), ())), preferred_element_type=F32)


def time_embed(step_index, width):
    half_width = width // 2
    frequency = jnp.exp(-math.log(10000.0) * jnp.arange(half_width, dtype=F32) / half_width)
    angles = (step_index[0].astype(F32) * frequency).reshape(1, half_width)
    return jnp.cos(angles), jnp.sin(angles)


def column_of(row):
    count = row.shape[1]
    diagonal = lax.broadcasted_iota(jnp.int32, (count, count), 0) == lax.broadcasted_iota(
        jnp.int32, (count, count), 1
    )
    return jnp.sum(jnp.where(diagonal, row.astype(F32), 0.0), axis=1, keepdims=True)


def encode_kernel(step_ref, earlier_ref, partial_ref, weight_ref, latent_ref, noise_ref, tail_ref, out_ref):
    frames, pixels, _ = partial_ref.shape
    lat = noise_ref.shape[1]
    patch = lat * 4
    cells = pixels // 4
    taps = weight_ref.shape[0] + 1
    step = jnp.full((lat, pixels), step_ref[0].astype(F32), F32)
    sigma = (STEPS - step) / STEPS
    row = lax.broadcasted_iota(jnp.int32, (lat, frames * patch), 0)
    lane = lax.broadcasted_iota(jnp.int32, (lat, frames * patch), 1)
    pixel = lax.broadcasted_iota(jnp.int32, (pixels, frames * patch), 0)
    feature = lax.broadcasted_iota(jnp.int32, (pixels, frames * patch), 1)
    keep = (pixel % 4) == (feature % 4)
    collect = (
        lax.broadcasted_iota(jnp.int32, (cells, pixels), 1) // 4
        == lax.broadcasted_iota(jnp.int32, (cells, pixels), 0)
    ).astype(BF16)
    patches = jnp.zeros((cells, frames * patch), F32)
    for t in range(frames):
        total = partial_ref[t]
        for tap in range(t + 1, taps):
            total = total + dot_rows(earlier_ref[frames + t - tap], weight_ref[tap - 1])
        hidden = (total / (1.0 + jnp.exp(-total))).astype(BF16)
        mixed = dot_rows(latent_ref[...], hidden)
        noisy = ((1.0 - sigma) * mixed + sigma * noise_ref[t].astype(F32)).astype(BF16)
        spread = (lane // 4 == row + t * lat).astype(BF16)
        wide = lax.dot_general(noisy, spread, (((0,), (0,)), ((), ())), preferred_element_type=F32)
        wide = jnp.where(keep, wide, 0.0).astype(BF16)
        patches = patches + dot(collect, wide)
    out_ref[0:cells, :] = patches.astype(BF16)
    out_ref[cells:, :] = tail_ref[...]


def exact_parts(values):
    high = values.astype(BF16)
    rest = values - high.astype(F32)
    middle = rest.astype(BF16)
    return high, middle, (rest - middle.astype(F32)).astype(BF16)


def prepare_kernel(
    w_in_ref, cos_ref, sin_ref, feats_ref, weight_ref, bias_ref, latent_ref, noise_ref, hist_ref, level_ref,
    wide_ref, gram_ref, partial_ref, taps_ref, latent_out_ref, noise_out_ref, tail_ref,
):
    frames, pixels, channels = feats_ref.shape
    for t in range(frames):
        total = jnp.broadcast_to(bias_ref[...], (pixels, channels))
        for tap in range(t + 1):
            total = total + dot_rows(feats_ref[t - tap], weight_ref[tap])
        partial_ref[t] = total
    taps_ref[...] = weight_ref[1:]
    latent_out_ref[...] = latent_ref[...]
    noise_out_ref[...] = noise_ref[...]
    patch, width = w_in_ref.shape
    slots = hist_ref.shape[0]
    level = jnp.broadcast_to(column_of(level_ref[...]), (slots, patch))
    tail = jnp.concatenate([hist_ref[...].astype(F32), level], axis=1)
    rest = jnp.zeros((tail_ref.shape[0] - slots, 2 * patch), F32)
    tail_ref[...] = jnp.concatenate([tail, rest], axis=0).astype(BF16)
    lanes = wide_ref.shape[0]
    for n, source in ((0, cos_ref), (width // 2, sin_ref)):
        values = source[...]
        row = lax.broadcasted_iota(jnp.int32, (lanes - patch, values.shape[1]), 0)
        high, middle, low = exact_parts(values)
        extra = jnp.where(row == 0, high.astype(F32), 0.0)
        extra = jnp.where(row == 1, middle.astype(F32), extra)
        extra = jnp.where(row == 2, low.astype(F32), extra)
        wide_ref[patch:lanes, n : n + values.shape[1]] = extra.astype(BF16)
    wide_ref[0:patch, :] = w_in_ref[...]
    gram = jnp.zeros((lanes, lanes), F32)
    step = 512
    for n in range(0, width, step):
        part = wide_ref[:, n : n + step]
        gram = gram + dot_rows(part, part)
    for number, part in enumerate(exact_parts(gram)):
        gram_ref[number * lanes : (number + 1) * lanes, :] = part


def joint_kernel(*refs, cells, block, pieces, owner_masks, tile, query_rows):
    near, far = refs[:pieces], refs[pieces : 2 * pieces]
    (
        count_ref, wide_ref, gram_ref, w_hist_ref, gain_ref, w_query_ref, w_key_ref, w_value_ref,
        q_gain_ref, k_gain_ref, hist_ref, own_ref, sib_ref,
        patch_ref, w_q_ref, w_kv_ref, tok_a_ref, tok_b_ref, q_ref, k_ref, v_ref, s_a_ref,
        s_b_ref, x_ref, out_ref, semaphores,
    ) = refs[2 * pieces :]
    heads, _, size = k_ref.shape
    levels, patch, width = w_hist_ref.shape
    depth = heads * size
    lanes = near[0].shape[1]
    frames = lanes // patch
    rows = 4 * cells * frames
    group = lax.axis_index("grp")
    place = lax.axis_index("seq")
    start = pl.multiple_of((place % 2) * depth, depth)
    copies = [
        pltpu.make_async_copy(w_query_ref.at[:, pl.ds(start, depth)], w_q_ref, semaphores.at[0]),
        pltpu.make_async_copy(
            w_key_ref.at[:, pl.ds(start, depth)], w_kv_ref.at[:, 0:depth], semaphores.at[1]
        ),
        pltpu.make_async_copy(
            w_value_ref.at[:, pl.ds(start, depth)], w_kv_ref.at[:, depth : 2 * depth], semaphores.at[2]
        ),
    ]
    for copy in copies:
        copy.start()

    step = 512
    lane = lax.broadcasted_iota(jnp.int32, (1, lanes), 1)
    ones = jnp.where(lane < patch + 3, 1.0, 0.0)
    held = near[0].shape[0] // block
    half = pieces * held
    fours = []
    for sources in (near, far):
        mine = sources[0][0:cells, :]
        theirs = sources[pieces // 2][0:cells, :]
        fours.append(jnp.where(group == 0, mine, theirs))
        fours.append(jnp.where(group == 0, theirs, mine))
    for sources in (near, far):
        for p in range(half):
            if p != 0 and p != half // 2:
                fours.append((sources[p // held], (p % held) * block))
    for spot, item in enumerate(fours):
        values = (item[0][item[1] : item[1] + cells, :] if isinstance(item, tuple) else item).astype(F32)
        for t in range(frames):
            moved = values if t == 0 else pltpu.roll(values, lanes - t * patch, 1)
            at = (spot // 4) * rows + t * 4 * cells + (spot % 4) * cells
            patch_ref[at : at + cells, :] = jnp.where(lane < patch, moved, ones).astype(BF16)

    def tokens_of(at, count, tok_ref):
        source = patch_ref[pl.ds(at, count), :]
        mixed = dot(jnp.concatenate([source] * 3, axis=1), gram_ref[...])
        mean = jnp.sum(mixed * source.astype(F32), axis=1, keepdims=True) / width
        inverse = lax.rsqrt(mean + EPSILON)
        for n in range(0, width, step):
            x = dot(source, wide_ref[:, n : n + step])
            tok_ref[0:count, n : n + step] = (x * inverse * gain_ref[:, n : n + step]).astype(BF16)

    def head_norm(values, gain):
        mean = jnp.mean(values * values, axis=1, keepdims=True)
        return (values * lax.rsqrt(mean + EPSILON) * gain).astype(BF16)

    def project(tokens, at):
        both = dot(tokens, w_kv_ref[...])
        count = tokens.shape[0]
        for h in range(heads):
            k_ref[h, pl.ds(at, count), :] = head_norm(both[:, h * size : (h + 1) * size], k_gain_ref[...])
            v_ref[h, pl.ds(at, count), :] = both[:, (heads + h) * size : (heads + h + 1) * size].astype(BF16)

    tokens_of(0, rows, tok_a_ref)
    for copy in copies:
        copy.wait()
    tokens_of(rows, tile, tok_b_ref)
    q = dot(tok_a_ref[0:rows, :], w_q_ref[...])
    for h in range(heads):
        q_ref[h] = head_norm(q[:, h * size : (h + 1) * size], q_gain_ref[...])
    project(tok_a_ref[0:rows, :], 0)
    section = patch_ref.shape[0]

    def pair(j, carry):
        at = pl.multiple_of(rows + 2 * j * tile, rows)
        tokens_of(at + tile, tile, tok_a_ref)
        project(tok_b_ref[...], at)
        tokens_of(at + 2 * tile, tile, tok_b_ref)
        project(tok_a_ref[...], at + tile)
        return carry

    pairs = (section - 2 * rows) // tile // 2
    if pairs == 1:
        pair(0, 0)
    elif pairs > 1:
        lax.fori_loop(0, pairs, pair, 0)
    tokens_of(section - rows, rows, tok_a_ref)
    project(tok_b_ref[...], section - rows - tile)
    project(tok_a_ref[0:rows, :], section - rows)

    slots = hist_ref.shape[0]
    owners = len(owner_masks)
    spread = 128 // slots
    owner_blocks = [
        (sources[p // held], (p % held) * block + cells) for sources in (near, far) for p in range(half // 2)
    ]
    biases = []
    for r in range(0, owners, spread):
        taken = owner_blocks[r : r + spread]
        source = jnp.concatenate([ref[at : at + 16, :].astype(F32)[0:slots] for ref, at in taken], axis=0)
        count = source.shape[0]
        values, level = source[:, 0:patch], source[:, patch : 2 * patch]
        parts = [jnp.where(level == v, values, 0.0).astype(BF16) for v in range(levels)]
        squares = jnp.zeros((count, 128), F32)
        for n in range(0, width, step):
            x = dot(parts[0], w_hist_ref[0, :, n : n + step])
            for v in range(1, levels):
                x = x + dot(parts[v], w_hist_ref[v, :, n : n + step])
            x_ref[0:count, n : n + step] = x
            for m in range(0, step, 128):
                squares = squares + x[:, m : m + 128] * x[:, m : m + 128]
        inverse = lax.rsqrt(jnp.sum(squares, axis=1, keepdims=True) / width + EPSILON)
        for n in range(0, width, step):
            tok_b_ref[0:count, n : n + step] = (
                x_ref[0:count, n : n + step] * inverse * gain_ref[:, n : n + step]
            ).astype(BF16)
        project(tok_b_ref[0:count, :], section + r * slots)
        slot = lax.broadcasted_iota(jnp.int32, (1, count), 1)
        live = jnp.zeros((1, count), jnp.int32)
        for o in range(len(taken)):
            live = jnp.where(slot // slots == o, count_ref[place ^ owner_masks[r + o]], live)
        biases.append(jnp.where(slot % slots < live, 0.0, -1e30))

    scale = math.log2(math.e) / math.sqrt(size)
    chunk = 512
    fold = 128
    parts = [(a, chunk, None) for a in range(0, section, chunk)]
    parts += [(section + r * spread * slots, b.shape[1], b) for r, b in enumerate(biases)]
    units = [(h, a) for h in range(heads) for a in range(0, rows, query_rows)]
    buffers = (s_a_ref, s_b_ref)

    def score(unit, state, part):
        h, a = units[unit]
        at, length, bias = part
        for n in range(at, at + length, 256):
            span = min(256, at + length - n)
            s = lax.dot_general(
                q_ref[h, a : a + query_rows, :], k_ref[h, n : n + span, :], (((1,), (1,)), ((), ())),
                preferred_element_type=F32,
            )
            if bias is not None:
                s = s + bias[:, n - at : n - at + span]
            buffers[unit % 2][:, n : n + span] = s
            for m in range(0, span, fold):
                state = jnp.maximum(state, s[:, m : m + fold])
        return state

    fresh = jnp.full((query_rows, fold), -3e38, F32)
    state = fresh
    for part in parts:
        state = score(0, state, part)
    for unit, (h, a) in enumerate(units):
        top = jnp.max(state, axis=1, keepdims=True)
        state = fresh
        total = jnp.zeros((query_rows, fold), F32)
        weighted = jnp.zeros((query_rows, size), F32)
        for part in parts:
            at, length, _ = part
            soft = jnp.exp2((buffers[unit % 2][:, at : at + length] - top) * scale)
            for m in range(0, length, fold):
                total = total + soft[:, m : m + fold]
            weighted = weighted + dot(soft.astype(BF16), v_ref[h, at : at + length, :])
            if unit + 1 < len(units):
                state = score(unit + 1, state, part)
        out_ref[a : a + query_rows, h * size : (h + 1) * size] = (
            weighted / jnp.sum(total, axis=1, keepdims=True)
        ).astype(BF16)
    part = 2 * cells
    for t in range(frames):
        base = t * 4 * cells
        own_ref[t * part : (t + 1) * part, :] = out_ref[base : base + part, :]
        sib_ref[t * part : (t + 1) * part, :] = out_ref[base + part : base + 2 * part, :]


def combine_local_kernel(own_ref, sib_ref, w_local_ref, total_ref):
    core = lax.axis_index("seq") % 2
    depth = own_ref.shape[1]
    mine = pl.ds(pl.multiple_of(core * depth, depth), depth)
    other = pl.ds(pl.multiple_of((1 - core) * depth, depth), depth)
    step = 512
    for n in range(0, total_ref.shape[1], step):
        columns = slice(n, n + step)
        total = dot(own_ref[...], w_local_ref[mine, columns])
        total_ref[:, columns] = total + dot(sib_ref[...], w_local_ref[other, columns])


def combine_kernel(total_ref, across_ref, corner_ref, w_across_ref, w_corner_ref, out_ref, held_ref, semaphores):
    step = 512
    copies = []
    for number, n in enumerate(range(0, held_ref.shape[1], step)):
        columns = slice(n, n + step)
        total = total_ref[:, columns] + dot(across_ref[...], w_across_ref[:, columns])
        total = total + dot(corner_ref[...], w_corner_ref[:, columns])
        held_ref[:, columns] = total.astype(BF16)
        copies.append(
            pltpu.make_async_copy(held_ref.at[:, columns], out_ref.at[:, columns], semaphores.at[number])
        )
        copies[-1].start()
    for copy in copies:
        copy.wait()


def in_hbm(*values):
    return [pltpu.with_memory_space_constraint(value, pltpu.HBM) for value in values]


def flip(value, mask, seq_count):
    pairs = [(i, i ^ mask) for i in range(2 * seq_count)]
    return lax.ppermute(value, ("grp", "seq"), pairs)


def local(
    feats, conv_weight, conv_bias, latent_projection_weight, noise, step_index, hist, hist_level,
    hist_count, w_in, w_hist, norm_gain, w_query, w_key, w_value, q_gain, k_gain, w_out,
):
    frame_count, channels, pixels = feats.shape
    seq_count = lax.axis_size("seq")
    group = lax.axis_index("grp")
    place = lax.axis_index("seq")
    core = place % 2
    width = w_in.shape[1]
    patch = w_in.shape[0]
    cells = pixels // 4
    slots = hist.shape[0]
    block = cells + 16
    lanes = frame_count * patch
    size = q_gain.shape[0]
    heads = w_query.shape[1] // size // 2
    depth = heads * size

    swapped = feats.transpose(0, 2, 1)
    earlier = lax.ppermute(swapped, "seq", [(i, i + 1) for i in range(seq_count - 1)])
    cos, sin = time_embed(step_index, width)
    wide, gram, partial, taps, latent, held_noise, tail = pl.pallas_call(
        prepare_kernel,
        out_shape=[
            jax.ShapeDtypeStruct((lanes, width), BF16),
            jax.ShapeDtypeStruct((3 * lanes, lanes), BF16),
            jax.ShapeDtypeStruct(swapped.shape, F32),
            jax.ShapeDtypeStruct((conv_weight.shape[0] - 1,) + conv_weight.shape[1:], BF16),
            jax.ShapeDtypeStruct(latent_projection_weight.shape, BF16),
            jax.ShapeDtypeStruct(noise.shape, BF16),
            jax.ShapeDtypeStruct((block - cells, lanes), BF16),
        ],
        in_specs=[VMEM] * 10,
        out_specs=[VMEM] * 7,
        compiler_params=pltpu.CompilerParams(vmem_limit_bytes=10 * 2**20),
        name="prepare",
    )(
        *in_hbm(
            w_in, cos, sin, swapped, conv_weight, conv_bias.reshape(1, channels),
            latent_projection_weight, noise, hist, hist_level.reshape(1, slots),
        )
    )
    earlier, partial = lax.optimization_barrier((earlier, partial))
    gathered = pl.pallas_call(
        encode_kernel,
        out_shape=jax.ShapeDtypeStruct((block, lanes), BF16),
        in_specs=[SMEM] + [VMEM] * 6,
        out_specs=VMEM,
        compiler_params=pltpu.CompilerParams(vmem_limit_bytes=6 * 2**20),
        name="encode",
    )(step_index, earlier, partial, taps, latent, held_noise, tail)
    columns = w_out.shape[1] // 2
    w_send = lax.dynamic_slice(w_out, (core * depth, (1 - group) * columns), (depth, columns))

    bits = []
    bit = seq_count // 2
    while bit > 1:
        bits.append(bit)
        bit //= 2
    owner_masks = [0]
    for bit in bits:
        owner_masks = owner_masks + [m ^ bit for m in owner_masks]
    owner_masks = tuple(owner_masks + [m ^ 1 for m in owner_masks])
    bits.append(seq_count)
    rounds = [bits[i : i + 2] for i in range(len(bits) % 2, len(bits), 2)]
    if len(bits) % 2:
        rounds = [bits[:1]] + rounds
    for number, pair in enumerate(rounds):
        masks = [0] + [pair[0]] + ([pair[1], pair[0] ^ pair[1]] if len(pair) > 1 else [])
        near = [gathered] + [flip(gathered, mask, seq_count) for mask in masks[1:]]
        if number + 1 < len(rounds):
            gathered = jnp.concatenate(near, axis=0)
            gathered, w_send = lax.optimization_barrier((gathered, w_send))
    far = [flip(near[0], 1, seq_count)]
    far += [flip(piece, 1, seq_count) for piece in near[1:]]

    w_across = flip(w_send, seq_count, seq_count)
    w_local = lax.dynamic_slice_in_dim(w_out, group * columns, columns, axis=1)

    tokens = 2 * seq_count * frame_count * cells
    keys = tokens + slots * seq_count
    rows = frame_count * 4 * cells
    tile = 2 * rows
    query_rows = rows
    while 2 * query_rows * keys * 4 > 12 * 2**20:
        query_rows //= 2
    limit = (
        2 * tokens * lanes + 6 * width * depth + 4 * tile * width + 4 * keys * depth
        + 8 * query_rows * keys + 512 * width + 4 * rows * depth + 12 * 2**20
    )
    anywhere = pl.BlockSpec(memory_space=pltpu.HBM)
    own, sib = pl.pallas_call(
        functools.partial(
            joint_kernel, cells=cells, block=block, pieces=len(near), owner_masks=owner_masks, tile=tile,
            query_rows=query_rows,
        ),
        out_shape=[jax.ShapeDtypeStruct((rows // 2, depth), BF16)] * 2,
        in_specs=[VMEM] * (2 * len(near)) + [SMEM] + [VMEM] * 4 + [anywhere] * 3 + [VMEM] * 3,
        out_specs=[VMEM] * 2,
        scratch_shapes=[
            pltpu.VMEM((tokens, lanes), BF16),
            pltpu.VMEM((width, depth), BF16),
            pltpu.VMEM((width, 2 * depth), BF16),
            pltpu.VMEM((tile, width), BF16),
            pltpu.VMEM((tile, width), BF16),
            pltpu.VMEM((heads, rows, size), BF16),
            pltpu.VMEM((heads, keys, size), BF16),
            pltpu.VMEM((heads, keys, size), BF16),
            pltpu.VMEM((query_rows, keys), F32),
            pltpu.VMEM((query_rows, keys), F32),
            pltpu.VMEM((128, width), F32),
            pltpu.VMEM((rows, depth), BF16),
            pltpu.SemaphoreType.DMA((3,)),
        ],
        compiler_params=pltpu.CompilerParams(vmem_limit_bytes=limit),
        cost_estimate=pl.CostEstimate(
            flops=2 * keys * width * 3 * depth + 4 * rows * keys * depth,
            bytes_accessed=6 * width * depth,
            transcendentals=rows * keys * heads,
        ),
        name="joint",
    )(
        *near, *far, hist_count, wide, gram, w_hist, norm_gain.reshape(1, width),
        *in_hbm(w_query, w_key, w_value), q_gain.reshape(1, size), k_gain.reshape(1, size), hist,
    )
    w_across, own, sib = lax.optimization_barrier((w_across, own, sib))
    w_corner = flip(w_across, 1, seq_count)
    from_sib = flip(sib, 1, seq_count)
    across = flip(own, seq_count, seq_count)
    corner = flip(sib, seq_count + 1, seq_count)
    total = pl.pallas_call(
        combine_local_kernel,
        out_shape=jax.ShapeDtypeStruct((rows // 2, columns), F32),
        in_specs=[VMEM] * 3,
        out_specs=VMEM,
        compiler_params=pltpu.CompilerParams(vmem_limit_bytes=10 * 2**20),
        name="combine_local",
    )(own, from_sib, w_local)
    return pl.pallas_call(
        combine_kernel,
        out_shape=jax.ShapeDtypeStruct((rows // 2, columns), BF16),
        in_specs=[VMEM] * 5,
        out_specs=anywhere,
        scratch_shapes=[
            pltpu.VMEM((rows // 2, columns), BF16), pltpu.SemaphoreType.DMA((columns // 512,))
        ],
        compiler_params=pltpu.CompilerParams(vmem_limit_bytes=10 * 2**20),
        name="combine",
    )(total, across, corner, w_across, w_corner)


def solution(mesh):
    placed = (
        P("seq", None, "grp"), P(), P(), P(), P("seq", None, "grp"), P(), P("seq", None), P("seq"),
        P(), P(), P(), P(), P(None, "grp"), P(None, "grp"), P(None, "grp"), P(), P(), P("grp", None),
    )
    return jax.shard_map(local, mesh=mesh, in_specs=placed, out_specs=P("seq", "grp"), check_vma=False)
```

```python
import functools
import math

import jax
import jax.numpy as jnp
from jax import lax
from jax.experimental import pallas as pl
from jax.experimental.pallas import tpu as pltpu
from jax.sharding import PartitionSpec as P


STEPS = 50
EPSILON = 1e-06
F32 = jnp.float32
BF16 = jnp.bfloat16
VMEM = pl.BlockSpec(memory_space=pltpu.VMEM)
SMEM = pl.BlockSpec(memory_space=pltpu.SMEM)


def dot(a, b):
    return jnp.dot(a, b, preferred_element_type=F32)


def dot_rows(a, b):
    return lax.dot_general(a, b, (((1,), (1,)), ((), ())), preferred_element_type=F32)


def time_embed(step_index, width):
    half_width = width // 2
    frequency = jnp.exp(-math.log(10000.0) * jnp.arange(half_width, dtype=F32) / half_width)
    angles = (step_index[0].astype(F32) * frequency).reshape(1, half_width)
    return jnp.cos(angles), jnp.sin(angles)


def column_of(row):
    count = row.shape[1]
    diagonal = lax.broadcasted_iota(jnp.int32, (count, count), 0) == lax.broadcasted_iota(
        jnp.int32, (count, count), 1
    )
    return jnp.sum(jnp.where(diagonal, row.astype(F32), 0.0), axis=1, keepdims=True)


def encode_kernel(step_ref, earlier_ref, partial_ref, weight_ref, latent_ref, noise_ref, tail_ref, out_ref):
    frames, pixels, _ = partial_ref.shape
    lat = noise_ref.shape[1]
    patch = lat * 4
    cells = pixels // 4
    taps = weight_ref.shape[0] + 1
    step = jnp.full((lat, pixels), step_ref[0].astype(F32), F32)
    sigma = (STEPS - step) / STEPS
    row = lax.broadcasted_iota(jnp.int32, (lat, frames * patch), 0)
    lane = lax.broadcasted_iota(jnp.int32, (lat, frames * patch), 1)
    pixel = lax.broadcasted_iota(jnp.int32, (pixels, frames * patch), 0)
    feature = lax.broadcasted_iota(jnp.int32, (pixels, frames * patch), 1)
    keep = (pixel % 4) == (feature % 4)
    collect = (
        lax.broadcasted_iota(jnp.int32, (cells, pixels), 1) // 4
        == lax.broadcasted_iota(jnp.int32, (cells, pixels), 0)
    ).astype(BF16)
    patches = jnp.zeros((cells, frames * patch), F32)
    for t in range(frames):
        total = partial_ref[t]
        for tap in range(t + 1, taps):
            total = total + dot_rows(earlier_ref[frames + t - tap], weight_ref[tap - 1])
        hidden = (total / (1.0 + jnp.exp(-total))).astype(BF16)
        mixed = dot_rows(latent_ref[...], hidden)
        noisy = ((1.0 - sigma) * mixed + sigma * noise_ref[t].astype(F32)).astype(BF16)
        spread = (lane // 4 == row + t * lat).astype(BF16)
        wide = lax.dot_general(noisy, spread, (((0,), (0,)), ((), ())), preferred_element_type=F32)
        wide = jnp.where(keep, wide, 0.0).astype(BF16)
        patches = patches + dot(collect, wide)
    out_ref[0:cells, :] = patches.astype(BF16)
    out_ref[cells:, :] = tail_ref[...]


def exact_parts(values):
    high = values.astype(BF16)
    rest = values - high.astype(F32)
    middle = rest.astype(BF16)
    return high, middle, (rest - middle.astype(F32)).astype(BF16)


def prepare_kernel(
    w_in_ref, cos_ref, sin_ref, feats_ref, weight_ref, bias_ref, latent_ref, noise_ref, hist_ref, level_ref,
    wide_ref, gram_ref, partial_ref, taps_ref, latent_out_ref, noise_out_ref, tail_ref,
):
    frames, pixels, channels = feats_ref.shape
    for t in range(frames):
        total = jnp.broadcast_to(bias_ref[...], (pixels, channels))
        for tap in range(t + 1):
            total = total + dot_rows(feats_ref[t - tap], weight_ref[tap])
        partial_ref[t] = total
    taps_ref[...] = weight_ref[1:]
    latent_out_ref[...] = latent_ref[...]
    noise_out_ref[...] = noise_ref[...]
    patch, width = w_in_ref.shape
    slots = hist_ref.shape[0]
    level = jnp.broadcast_to(column_of(level_ref[...]), (slots, patch))
    tail = jnp.concatenate([hist_ref[...].astype(F32), level], axis=1)
    rest = jnp.zeros((tail_ref.shape[0] - slots, 2 * patch), F32)
    tail_ref[...] = jnp.concatenate([tail, rest], axis=0).astype(BF16)
    lanes = wide_ref.shape[0]
    for n, source in ((0, cos_ref), (width // 2, sin_ref)):
        values = source[...]
        row = lax.broadcasted_iota(jnp.int32, (lanes - patch, values.shape[1]), 0)
        high, middle, low = exact_parts(values)
        extra = jnp.where(row == 0, high.astype(F32), 0.0)
        extra = jnp.where(row == 1, middle.astype(F32), extra)
        extra = jnp.where(row == 2, low.astype(F32), extra)
        wide_ref[patch:lanes, n : n + values.shape[1]] = extra.astype(BF16)
    wide_ref[0:patch, :] = w_in_ref[...]
    gram = jnp.zeros((lanes, lanes), F32)
    step = 512
    for n in range(0, width, step):
        part = wide_ref[:, n : n + step]
        gram = gram + dot_rows(part, part)
    for number, part in enumerate(exact_parts(gram)):
        gram_ref[number * lanes : (number + 1) * lanes, :] = part


def joint_kernel(*refs, cells, block, pieces, owner_masks, tile, query_rows):
    near, far = refs[:pieces], refs[pieces : 2 * pieces]
    (
        count_ref, wide_ref, gram_ref, w_hist_ref, gain_ref, w_query_ref, w_key_ref, w_value_ref,
        q_gain_ref, k_gain_ref, hist_ref, own_ref, sib_ref,
        patch_ref, w_q_ref, w_kv_ref, tok_a_ref, tok_b_ref, q_ref, k_ref, v_ref, s_a_ref,
        s_b_ref, x_ref, out_ref, semaphores,
    ) = refs[2 * pieces :]
    heads, _, size = k_ref.shape
    levels, patch, width = w_hist_ref.shape
    depth = heads * size
    lanes = near[0].shape[1]
    frames = lanes // patch
    rows = 4 * cells * frames
    group = lax.axis_index("grp")
    place = lax.axis_index("seq")
    start = pl.multiple_of((place % 2) * depth, depth)
    copies = [
        pltpu.make_async_copy(w_query_ref.at[:, pl.ds(start, depth)], w_q_ref, semaphores.at[0]),
        pltpu.make_async_copy(
            w_key_ref.at[:, pl.ds(start, depth)], w_kv_ref.at[:, 0:depth], semaphores.at[1]
        ),
        pltpu.make_async_copy(
            w_value_ref.at[:, pl.ds(start, depth)], w_kv_ref.at[:, depth : 2 * depth], semaphores.at[2]
        ),
    ]
    for copy in copies:
        copy.start()

    step = 512
    lane = lax.broadcasted_iota(jnp.int32, (1, lanes), 1)
    ones = jnp.where(lane < patch + 3, 1.0, 0.0)
    held = near[0].shape[0] // block
    half = pieces * held
    fours = []
    for sources in (near, far):
        mine = sources[0][0:cells, :]
        theirs = sources[pieces // 2][0:cells, :]
        fours.append(jnp.where(group == 0, mine, theirs))
        fours.append(jnp.where(group == 0, theirs, mine))
    for sources in (near, far):
        for p in range(half):
            if p != 0 and p != half // 2:
                fours.append((sources[p // held], (p % held) * block))
    for spot, item in enumerate(fours):
        values = (item[0][item[1] : item[1] + cells, :] if isinstance(item, tuple) else item).astype(F32)
        for t in range(frames):
            moved = values if t == 0 else pltpu.roll(values, lanes - t * patch, 1)
            at = (spot // 4) * rows + t * 4 * cells + (spot % 4) * cells
            patch_ref[at : at + cells, :] = jnp.where(lane < patch, moved, ones).astype(BF16)

    def tokens_of(i, tok_ref):
        source = patch_ref[pl.ds(pl.multiple_of(i * tile, tile), tile), :]
        mixed = dot(jnp.concatenate([source] * 3, axis=1), gram_ref[...])
        mean = jnp.sum(mixed * source.astype(F32), axis=1, keepdims=True) / width
        inverse = lax.rsqrt(mean + EPSILON)
        for n in range(0, width, step):
            x = dot(source, wide_ref[:, n : n + step])
            tok_ref[:, n : n + step] = (x * inverse * gain_ref[:, n : n + step]).astype(BF16)

    def head_norm(values, gain):
        mean = jnp.mean(values * values, axis=1, keepdims=True)
        return (values * lax.rsqrt(mean + EPSILON) * gain).astype(BF16)

    def project(tokens, at):
        both = dot(tokens, w_kv_ref[...])
        count = tokens.shape[0]
        for h in range(heads):
            k_ref[h, pl.ds(at, count), :] = head_norm(both[:, h * size : (h + 1) * size], k_gain_ref[...])
            v_ref[h, pl.ds(at, count), :] = both[:, (heads + h) * size : (heads + h + 1) * size].astype(BF16)

    tokens_of(0, tok_a_ref)
    for copy in copies:
        copy.wait()
    q = dot(tok_a_ref[0:rows, :], w_q_ref[...])
    for h in range(heads):
        q_ref[h] = head_norm(q[:, h * size : (h + 1) * size], q_gain_ref[...])
    tiles = patch_ref.shape[0] // tile

    def pair(j, carry):
        tokens_of(2 * j + 1, tok_b_ref)
        project(tok_a_ref[...], pl.multiple_of(2 * j * tile, tile))
        tokens_of(2 * j + 2, tok_a_ref)
        project(tok_b_ref[...], pl.multiple_of((2 * j + 1) * tile, tile))
        return carry

    if tiles > 2:
        lax.fori_loop(0, tiles // 2 - 1, pair, 0)
    tokens_of(tiles - 1, tok_b_ref)
    project(tok_a_ref[...], (tiles - 2) * tile)
    project(tok_b_ref[...], (tiles - 1) * tile)

    section = tiles * tile
    slots = hist_ref.shape[0]
    owners = len(owner_masks)
    spread = 128 // slots
    owner_blocks = [
        (sources[p // held], (p % held) * block + cells) for sources in (near, far) for p in range(half // 2)
    ]
    biases = []
    for r in range(0, owners, spread):
        taken = owner_blocks[r : r + spread]
        source = jnp.concatenate([ref[at : at + 16, :].astype(F32)[0:slots] for ref, at in taken], axis=0)
        count = source.shape[0]
        values, level = source[:, 0:patch], source[:, patch : 2 * patch]
        parts = [jnp.where(level == v, values, 0.0).astype(BF16) for v in range(levels)]
        squares = jnp.zeros((count, 128), F32)
        for n in range(0, width, step):
            x = dot(parts[0], w_hist_ref[0, :, n : n + step])
            for v in range(1, levels):
                x = x + dot(parts[v], w_hist_ref[v, :, n : n + step])
            x_ref[0:count, n : n + step] = x
            for m in range(0, step, 128):
                squares = squares + x[:, m : m + 128] * x[:, m : m + 128]
        inverse = lax.rsqrt(jnp.sum(squares, axis=1, keepdims=True) / width + EPSILON)
        for n in range(0, width, step):
            tok_a_ref[0:count, n : n + step] = (
                x_ref[0:count, n : n + step] * inverse * gain_ref[:, n : n + step]
            ).astype(BF16)
        project(tok_a_ref[0:count, :], section + r * slots)
        slot = lax.broadcasted_iota(jnp.int32, (1, count), 1)
        live = jnp.zeros((1, count), jnp.int32)
        for o in range(len(taken)):
            live = jnp.where(slot // slots == o, count_ref[place ^ owner_masks[r + o]], live)
        biases.append(jnp.where(slot % slots < live, 0.0, -1e30))

    scale = math.log2(math.e) / math.sqrt(size)
    chunk = 512
    fold = 128
    parts = [(a, chunk, None) for a in range(0, section, chunk)]
    parts += [(section + r * spread * slots, b.shape[1], b) for r, b in enumerate(biases)]
    units = [(h, a) for h in range(heads) for a in range(0, rows, query_rows)]
    buffers = (s_a_ref, s_b_ref)

    def score(unit, state, part):
        h, a = units[unit]
        at, length, bias = part
        for n in range(at, at + length, 256):
            span = min(256, at + length - n)
            s = lax.dot_general(
                q_ref[h, a : a + query_rows, :], k_ref[h, n : n + span, :], (((1,), (1,)), ((), ())),
                preferred_element_type=F32,
            )
            if bias is not None:
                s = s + bias[:, n - at : n - at + span]
            buffers[unit % 2][:, n : n + span] = s
            for m in range(0, span, fold):
                state = jnp.maximum(state, s[:, m : m + fold])
        return state

    fresh = jnp.full((query_rows, fold), -3e38, F32)
    state = fresh
    for part in parts:
        state = score(0, state, part)
    for unit, (h, a) in enumerate(units):
        top = jnp.max(state, axis=1, keepdims=True)
        state = fresh
        total = jnp.zeros((query_rows, fold), F32)
        weighted = jnp.zeros((query_rows, size), F32)
        for part in parts:
            at, length, _ = part
            soft = jnp.exp2((buffers[unit % 2][:, at : at + length] - top) * scale)
            for m in range(0, length, fold):
                total = total + soft[:, m : m + fold]
            weighted = weighted + dot(soft.astype(BF16), v_ref[h, at : at + length, :])
            if unit + 1 < len(units):
                state = score(unit + 1, state, part)
        out_ref[a : a + query_rows, h * size : (h + 1) * size] = (
            weighted / jnp.sum(total, axis=1, keepdims=True)
        ).astype(BF16)
    part = 2 * cells
    for t in range(frames):
        base = t * 4 * cells
        own_ref[t * part : (t + 1) * part, :] = out_ref[base : base + part, :]
        sib_ref[t * part : (t + 1) * part, :] = out_ref[base + part : base + 2 * part, :]


def combine_local_kernel(own_ref, sib_ref, w_local_ref, total_ref):
    core = lax.axis_index("seq") % 2
    depth = own_ref.shape[1]
    mine = pl.ds(pl.multiple_of(core * depth, depth), depth)
    other = pl.ds(pl.multiple_of((1 - core) * depth, depth), depth)
    step = 512
    for n in range(0, total_ref.shape[1], step):
        columns = slice(n, n + step)
        total = dot(own_ref[...], w_local_ref[mine, columns])
        total_ref[:, columns] = total + dot(sib_ref[...], w_local_ref[other, columns])


def combine_kernel(total_ref, across_ref, corner_ref, w_across_ref, w_corner_ref, out_ref, held_ref, semaphores):
    step = 512
    copies = []
    for number, n in enumerate(range(0, held_ref.shape[1], step)):
        columns = slice(n, n + step)
        total = total_ref[:, columns] + dot(across_ref[...], w_across_ref[:, columns])
        total = total + dot(corner_ref[...], w_corner_ref[:, columns])
        held_ref[:, columns] = total.astype(BF16)
        copies.append(
            pltpu.make_async_copy(held_ref.at[:, columns], out_ref.at[:, columns], semaphores.at[number])
        )
        copies[-1].start()
    for copy in copies:
        copy.wait()


def in_hbm(*values):
    return [pltpu.with_memory_space_constraint(value, pltpu.HBM) for value in values]


def flip(value, mask, seq_count):
    pairs = [(i, i ^ mask) for i in range(2 * seq_count)]
    return lax.ppermute(value, ("grp", "seq"), pairs)


def local(
    feats, conv_weight, conv_bias, latent_projection_weight, noise, step_index, hist, hist_level,
    hist_count, w_in, w_hist, norm_gain, w_query, w_key, w_value, q_gain, k_gain, w_out,
):
    frame_count, channels, pixels = feats.shape
    seq_count = lax.axis_size("seq")
    group = lax.axis_index("grp")
    place = lax.axis_index("seq")
    core = place % 2
    width = w_in.shape[1]
    patch = w_in.shape[0]
    cells = pixels // 4
    slots = hist.shape[0]
    block = cells + 16
    lanes = frame_count * patch
    size = q_gain.shape[0]
    heads = w_query.shape[1] // size // 2
    depth = heads * size

    swapped = feats.transpose(0, 2, 1)
    earlier = lax.ppermute(swapped, "seq", [(i, i + 1) for i in range(seq_count - 1)])
    cos, sin = time_embed(step_index, width)
    wide, gram, partial, taps, latent, held_noise, tail = pl.pallas_call(
        prepare_kernel,
        out_shape=[
            jax.ShapeDtypeStruct((lanes, width), BF16),
            jax.ShapeDtypeStruct((3 * lanes, lanes), BF16),
            jax.ShapeDtypeStruct(swapped.shape, F32),
            jax.ShapeDtypeStruct((conv_weight.shape[0] - 1,) + conv_weight.shape[1:], BF16),
            jax.ShapeDtypeStruct(latent_projection_weight.shape, BF16),
            jax.ShapeDtypeStruct(noise.shape, BF16),
            jax.ShapeDtypeStruct((block - cells, lanes), BF16),
        ],
        in_specs=[VMEM] * 10,
        out_specs=[VMEM] * 7,
        compiler_params=pltpu.CompilerParams(vmem_limit_bytes=10 * 2**20),
        name="prepare",
    )(
        *in_hbm(
            w_in, cos, sin, swapped, conv_weight, conv_bias.reshape(1, channels),
            latent_projection_weight, noise, hist, hist_level.reshape(1, slots),
        )
    )
    earlier, partial = lax.optimization_barrier((earlier, partial))
    gathered = pl.pallas_call(
        encode_kernel,
        out_shape=jax.ShapeDtypeStruct((block, lanes), BF16),
        in_specs=[SMEM] + [VMEM] * 6,
        out_specs=VMEM,
        compiler_params=pltpu.CompilerParams(vmem_limit_bytes=6 * 2**20),
        name="encode",
    )(step_index, earlier, partial, taps, latent, held_noise, tail)
    columns = w_out.shape[1] // 2
    w_send = lax.dynamic_slice(w_out, (core * depth, (1 - group) * columns), (depth, columns))

    bits = []
    bit = seq_count // 2
    while bit > 1:
        bits.append(bit)
        bit //= 2
    owner_masks = [0]
    for bit in bits:
        owner_masks = owner_masks + [m ^ bit for m in owner_masks]
    owner_masks = tuple(owner_masks + [m ^ 1 for m in owner_masks])
    bits.append(seq_count)
    rounds = [bits[i : i + 2] for i in range(len(bits) % 2, len(bits), 2)]
    if len(bits) % 2:
        rounds = [bits[:1]] + rounds
    for number, pair in enumerate(rounds):
        masks = [0] + [pair[0]] + ([pair[1], pair[0] ^ pair[1]] if len(pair) > 1 else [])
        near = [gathered]
        for mask in masks[1:]:
            near.append(flip(gathered, mask, seq_count))
        if number + 1 < len(rounds):
            gathered = jnp.concatenate(near, axis=0)
            gathered, w_send = lax.optimization_barrier((gathered, w_send))
    far = [flip(near[0], 1, seq_count)]
    far += [flip(piece, 1, seq_count) for piece in near[1:]]

    w_across = flip(w_send, seq_count, seq_count)
    w_local = lax.dynamic_slice_in_dim(w_out, group * columns, columns, axis=1)

    tokens = 2 * seq_count * frame_count * cells
    keys = tokens + slots * seq_count
    rows = frame_count * 4 * cells
    tile = 2 * rows
    query_rows = rows
    while 2 * query_rows * keys * 4 > 12 * 2**20:
        query_rows //= 2
    limit = (
        2 * tokens * lanes + 6 * width * depth + 4 * tile * width + 4 * keys * depth
        + 8 * query_rows * keys + 512 * width + 4 * rows * depth + 12 * 2**20
    )
    anywhere = pl.BlockSpec(memory_space=pltpu.HBM)
    own, sib = pl.pallas_call(
        functools.partial(
            joint_kernel, cells=cells, block=block, pieces=len(near), owner_masks=owner_masks, tile=tile,
            query_rows=query_rows,
        ),
        out_shape=[jax.ShapeDtypeStruct((rows // 2, depth), BF16)] * 2,
        in_specs=[VMEM] * (2 * len(near)) + [SMEM] + [VMEM] * 4 + [anywhere] * 3 + [VMEM] * 3,
        out_specs=[VMEM] * 2,
        scratch_shapes=[
            pltpu.VMEM((tokens, lanes), BF16),
            pltpu.VMEM((width, depth), BF16),
            pltpu.VMEM((width, 2 * depth), BF16),
            pltpu.VMEM((tile, width), BF16),
            pltpu.VMEM((tile, width), BF16),
            pltpu.VMEM((heads, rows, size), BF16),
            pltpu.VMEM((heads, keys, size), BF16),
            pltpu.VMEM((heads, keys, size), BF16),
            pltpu.VMEM((query_rows, keys), F32),
            pltpu.VMEM((query_rows, keys), F32),
            pltpu.VMEM((128, width), F32),
            pltpu.VMEM((rows, depth), BF16),
            pltpu.SemaphoreType.DMA((3,)),
        ],
        compiler_params=pltpu.CompilerParams(vmem_limit_bytes=limit),
        cost_estimate=pl.CostEstimate(
            flops=2 * keys * width * 3 * depth + 4 * rows * keys * depth,
            bytes_accessed=6 * width * depth,
            transcendentals=rows * keys * heads,
        ),
        name="joint",
    )(
        *near, *far, hist_count, wide, gram, w_hist, norm_gain.reshape(1, width),
        *in_hbm(w_query, w_key, w_value), q_gain.reshape(1, size), k_gain.reshape(1, size), hist,
    )
    w_across, own, sib = lax.optimization_barrier((w_across, own, sib))
    w_corner = flip(w_across, 1, seq_count)
    from_sib = flip(sib, 1, seq_count)
    across = flip(own, seq_count, seq_count)
    corner = flip(sib, seq_count + 1, seq_count)
    total = pl.pallas_call(
        combine_local_kernel,
        out_shape=jax.ShapeDtypeStruct((rows // 2, columns), F32),
        in_specs=[VMEM] * 3,
        out_specs=VMEM,
        compiler_params=pltpu.CompilerParams(vmem_limit_bytes=10 * 2**20),
        name="combine_local",
    )(own, from_sib, w_local)
    return pl.pallas_call(
        combine_kernel,
        out_shape=jax.ShapeDtypeStruct((rows // 2, columns), BF16),
        in_specs=[VMEM] * 5,
        out_specs=anywhere,
        scratch_shapes=[
            pltpu.VMEM((rows // 2, columns), BF16), pltpu.SemaphoreType.DMA((columns // 512,))
        ],
        compiler_params=pltpu.CompilerParams(vmem_limit_bytes=10 * 2**20),
        name="combine",
    )(total, across, corner, w_across, w_corner)


def solution(mesh):
    placed = (
        P("seq", None, "grp"), P(), P(), P(), P("seq", None, "grp"), P(), P("seq", None), P("seq"),
        P(), P(), P(), P(), P(None, "grp"), P(None, "grp"), P(None, "grp"), P(), P(), P("grp", None),
    )
    return jax.shard_map(local, mesh=mesh, in_specs=placed, out_specs=P("seq", "grp"), check_vma=False)
```

```python
import functools
import math

import jax
import jax.numpy as jnp
from jax import lax
from jax.experimental import pallas as pl
from jax.experimental.pallas import tpu as pltpu
from jax.sharding import PartitionSpec as P


STEPS = 50
EPSILON = 1e-06
F32 = jnp.float32
BF16 = jnp.bfloat16
VMEM = pl.BlockSpec(memory_space=pltpu.VMEM)
SMEM = pl.BlockSpec(memory_space=pltpu.SMEM)


def dot(a, b):
    return jnp.dot(a, b, preferred_element_type=F32)


def dot_rows(a, b):
    return lax.dot_general(a, b, (((1,), (1,)), ((), ())), preferred_element_type=F32)


def time_embed(step_index, width):
    half_width = width // 2
    frequency = jnp.exp(-math.log(10000.0) * jnp.arange(half_width, dtype=F32) / half_width)
    angles = (step_index[0].astype(F32) * frequency).reshape(1, half_width)
    return jnp.cos(angles), jnp.sin(angles)


def column_of(row):
    count = row.shape[1]
    diagonal = lax.broadcasted_iota(jnp.int32, (count, count), 0) == lax.broadcasted_iota(
        jnp.int32, (count, count), 1
    )
    return jnp.sum(jnp.where(diagonal, row.astype(F32), 0.0), axis=1, keepdims=True)


def encode_kernel(step_ref, earlier_ref, partial_ref, weight_ref, latent_ref, noise_ref, tail_ref, out_ref):
    frames, pixels, _ = partial_ref.shape
    lat = noise_ref.shape[1]
    patch = lat * 4
    cells = pixels // 4
    taps = weight_ref.shape[0] + 1
    step = jnp.full((lat, pixels), step_ref[0].astype(F32), F32)
    sigma = (STEPS - step) / STEPS
    row = lax.broadcasted_iota(jnp.int32, (lat, frames * patch), 0)
    lane = lax.broadcasted_iota(jnp.int32, (lat, frames * patch), 1)
    pixel = lax.broadcasted_iota(jnp.int32, (pixels, frames * patch), 0)
    feature = lax.broadcasted_iota(jnp.int32, (pixels, frames * patch), 1)
    keep = (pixel % 4) == (feature % 4)
    collect = (
        lax.broadcasted_iota(jnp.int32, (cells, pixels), 1) // 4
        == lax.broadcasted_iota(jnp.int32, (cells, pixels), 0)
    ).astype(BF16)
    patches = jnp.zeros((cells, frames * patch), F32)
    for t in range(frames):
        total = partial_ref[t]
        for tap in range(t + 1, taps):
            total = total + dot_rows(earlier_ref[frames + t - tap], weight_ref[tap - 1])
        hidden = (total / (1.0 + jnp.exp(-total))).astype(BF16)
        mixed = dot_rows(latent_ref[...], hidden)
        noisy = ((1.0 - sigma) * mixed + sigma * noise_ref[t].astype(F32)).astype(BF16)
        spread = (lane // 4 == row + t * lat).astype(BF16)
        wide = lax.dot_general(noisy, spread, (((0,), (0,)), ((), ())), preferred_element_type=F32)
        wide = jnp.where(keep, wide, 0.0).astype(BF16)
        patches = patches + dot(collect, wide)
    out_ref[0:cells, :] = patches.astype(BF16)
    out_ref[cells:, :] = tail_ref[...]


def exact_parts(values):
    high = values.astype(BF16)
    rest = values - high.astype(F32)
    middle = rest.astype(BF16)
    return high, middle, (rest - middle.astype(F32)).astype(BF16)


def prepare_kernel(
    w_in_ref, cos_ref, sin_ref, feats_ref, weight_ref, bias_ref, latent_ref, noise_ref, hist_ref, level_ref,
    wide_ref, gram_ref, partial_ref, taps_ref, latent_out_ref, noise_out_ref, tail_ref,
):
    frames, pixels, channels = feats_ref.shape
    for t in range(frames):
        total = jnp.broadcast_to(bias_ref[...], (pixels, channels))
        for tap in range(t + 1):
            total = total + dot_rows(feats_ref[t - tap], weight_ref[tap])
        partial_ref[t] = total
    taps_ref[...] = weight_ref[1:]
    latent_out_ref[...] = latent_ref[...]
    noise_out_ref[...] = noise_ref[...]
    patch, width = w_in_ref.shape
    slots = hist_ref.shape[0]
    level = jnp.broadcast_to(column_of(level_ref[...]), (slots, patch))
    tail = jnp.concatenate([hist_ref[...].astype(F32), level], axis=1)
    rest = jnp.zeros((tail_ref.shape[0] - slots, 2 * patch), F32)
    tail_ref[...] = jnp.concatenate([tail, rest], axis=0).astype(BF16)
    lanes = wide_ref.shape[0]
    for n, source in ((0, cos_ref), (width // 2, sin_ref)):
        values = source[...]
        row = lax.broadcasted_iota(jnp.int32, (lanes - patch, values.shape[1]), 0)
        high, middle, low = exact_parts(values)
        extra = jnp.where(row == 0, high.astype(F32), 0.0)
        extra = jnp.where(row == 1, middle.astype(F32), extra)
        extra = jnp.where(row == 2, low.astype(F32), extra)
        wide_ref[patch:lanes, n : n + values.shape[1]] = extra.astype(BF16)
    wide_ref[0:patch, :] = w_in_ref[...]
    gram = jnp.zeros((lanes, lanes), F32)
    step = 512
    for n in range(0, width, step):
        part = wide_ref[:, n : n + step]
        gram = gram + dot_rows(part, part)
    for number, part in enumerate(exact_parts(gram)):
        gram_ref[number * lanes : (number + 1) * lanes, :] = part


def fold_kernel(wide_ref, gain_ref, w_value_ref, folded_ref, w_v_ref, semaphore):
    depth = folded_ref.shape[1]
    lanes, width = wide_ref.shape
    start = pl.multiple_of((lax.axis_index("seq") % 2) * depth, depth)
    copy = pltpu.make_async_copy(w_value_ref.at[:, pl.ds(start, depth)], w_v_ref, semaphore)
    copy.start()
    copy.wait()
    total = jnp.zeros((lanes, depth), F32)
    step = 512
    for n in range(0, width, step):
        values = wide_ref[:, n : n + step].astype(F32) * gain_ref[:, n : n + step]
        stacked = jnp.concatenate(exact_parts(values), axis=0)
        product = dot(stacked, w_v_ref[n : n + step, :])
        total = total + (product[0:lanes] + (product[lanes : 2 * lanes] + product[2 * lanes :]))
    for number, part in enumerate(exact_parts(total)):
        folded_ref[number * lanes : (number + 1) * lanes, :] = part


def joint_kernel(*refs, cells, block, pieces, owner_masks, tile, query_rows):
    near, far = refs[:pieces], refs[pieces : 2 * pieces]
    (
        count_ref, wide_ref, gram_ref, folded_ref, w_v_ref, w_hist_ref, gain_ref, w_query_ref, w_key_ref,
        q_gain_ref, k_gain_ref, hist_ref, own_ref, sib_ref,
        patch_ref, w_q_ref, w_k_ref, tok_a_ref, tok_b_ref, q_ref, k_ref, v_ref, s_a_ref,
        s_b_ref, x_ref, out_ref, semaphores,
    ) = refs[2 * pieces :]
    heads, _, size = k_ref.shape
    levels, patch, width = w_hist_ref.shape
    depth = heads * size
    lanes = near[0].shape[1]
    frames = lanes // patch
    rows = 4 * cells * frames
    group = lax.axis_index("grp")
    place = lax.axis_index("seq")
    start = pl.multiple_of((place % 2) * depth, depth)
    copies = [
        pltpu.make_async_copy(w_query_ref.at[:, pl.ds(start, depth)], w_q_ref, semaphores.at[0]),
        pltpu.make_async_copy(w_key_ref.at[:, pl.ds(start, depth)], w_k_ref, semaphores.at[1]),
    ]
    for copy in copies:
        copy.start()

    step = 512
    lane = lax.broadcasted_iota(jnp.int32, (1, lanes), 1)
    ones = jnp.where(lane < patch + 3, 1.0, 0.0)
    held = near[0].shape[0] // block
    half = pieces * held
    fours = []
    for sources in (near, far):
        mine = sources[0][0:cells, :]
        theirs = sources[pieces // 2][0:cells, :]
        fours.append(jnp.where(group == 0, mine, theirs))
        fours.append(jnp.where(group == 0, theirs, mine))
    for sources in (near, far):
        for p in range(half):
            if p != 0 and p != half // 2:
                fours.append((sources[p // held], (p % held) * block))
    for spot, item in enumerate(fours):
        values = (item[0][item[1] : item[1] + cells, :] if isinstance(item, tuple) else item).astype(F32)
        for t in range(frames):
            moved = values if t == 0 else pltpu.roll(values, lanes - t * patch, 1)
            at = (spot // 4) * rows + t * 4 * cells + (spot % 4) * cells
            patch_ref[at : at + cells, :] = jnp.where(lane < patch, moved, ones).astype(BF16)

    def store_values(values, at):
        for h in range(heads):
            v_ref[h, pl.ds(at, values.shape[0]), :] = values[:, h * size : (h + 1) * size].astype(BF16)

    def tokens_of(i, tok_ref):
        source = patch_ref[pl.ds(pl.multiple_of(i * tile, tile), tile), :]
        tripled = jnp.concatenate([source] * 3, axis=1)
        mixed = dot(tripled, gram_ref[...])
        mean = jnp.sum(mixed * source.astype(F32), axis=1, keepdims=True) / width
        inverse = lax.rsqrt(mean + EPSILON)
        store_values(dot(tripled, folded_ref[...]) * inverse, pl.multiple_of(i * tile, tile))
        for n in range(0, width, step):
            x = dot(source, wide_ref[:, n : n + step])
            tok_ref[:, n : n + step] = (x * inverse * gain_ref[:, n : n + step]).astype(BF16)

    def head_norm(values, gain):
        mean = jnp.mean(values * values, axis=1, keepdims=True)
        return (values * lax.rsqrt(mean + EPSILON) * gain).astype(BF16)

    def project(tokens, at):
        found = dot(tokens, w_k_ref[...])
        for h in range(heads):
            k_ref[h, pl.ds(at, tokens.shape[0]), :] = head_norm(
                found[:, h * size : (h + 1) * size], k_gain_ref[...]
            )

    tokens_of(0, tok_a_ref)
    for copy in copies:
        copy.wait()
    q = dot(tok_a_ref[0:rows, :], w_q_ref[...])
    for h in range(heads):
        q_ref[h] = head_norm(q[:, h * size : (h + 1) * size], q_gain_ref[...])
    tiles = patch_ref.shape[0] // tile

    def pair(j, carry):
        tokens_of(2 * j + 1, tok_b_ref)
        project(tok_a_ref[...], pl.multiple_of(2 * j * tile, tile))
        tokens_of(2 * j + 2, tok_a_ref)
        project(tok_b_ref[...], pl.multiple_of((2 * j + 1) * tile, tile))
        return carry

    if tiles > 2:
        lax.fori_loop(0, tiles // 2 - 1, pair, 0)
    tokens_of(tiles - 1, tok_b_ref)
    project(tok_a_ref[...], (tiles - 2) * tile)
    project(tok_b_ref[...], (tiles - 1) * tile)

    section = tiles * tile
    slots = hist_ref.shape[0]
    owners = len(owner_masks)
    spread = 128 // slots
    owner_blocks = [
        (sources[p // held], (p % held) * block + cells) for sources in (near, far) for p in range(half // 2)
    ]
    biases = []
    for r in range(0, owners, spread):
        taken = owner_blocks[r : r + spread]
        source = jnp.concatenate([ref[at : at + 16, :].astype(F32)[0:slots] for ref, at in taken], axis=0)
        count = source.shape[0]
        values, level = source[:, 0:patch], source[:, patch : 2 * patch]
        parts = [jnp.where(level == v, values, 0.0).astype(BF16) for v in range(levels)]
        squares = jnp.zeros((count, 128), F32)
        for n in range(0, width, step):
            x = dot(parts[0], w_hist_ref[0, :, n : n + step])
            for v in range(1, levels):
                x = x + dot(parts[v], w_hist_ref[v, :, n : n + step])
            x_ref[0:count, n : n + step] = x
            for m in range(0, step, 128):
                squares = squares + x[:, m : m + 128] * x[:, m : m + 128]
        inverse = lax.rsqrt(jnp.sum(squares, axis=1, keepdims=True) / width + EPSILON)
        for n in range(0, width, step):
            tok_a_ref[0:count, n : n + step] = (
                x_ref[0:count, n : n + step] * inverse * gain_ref[:, n : n + step]
            ).astype(BF16)
        project(tok_a_ref[0:count, :], section + r * slots)
        store_values(dot(tok_a_ref[0:count, :], w_v_ref[...]), section + r * slots)
        slot = lax.broadcasted_iota(jnp.int32, (1, count), 1)
        live = jnp.zeros((1, count), jnp.int32)
        for o in range(len(taken)):
            live = jnp.where(slot // slots == o, count_ref[place ^ owner_masks[r + o]], live)
        biases.append(jnp.where(slot % slots < live, 0.0, -1e30))

    scale = math.log2(math.e) / math.sqrt(size)
    chunk = 512
    fold = 128
    parts = [(a, chunk, None) for a in range(0, section, chunk)]
    parts += [(section + r * spread * slots, b.shape[1], b) for r, b in enumerate(biases)]
    units = [(h, a) for h in range(heads) for a in range(0, rows, query_rows)]
    buffers = (s_a_ref, s_b_ref)

    def score(unit, state, part):
        h, a = units[unit]
        at, length, bias = part
        for n in range(at, at + length, 256):
            span = min(256, at + length - n)
            s = lax.dot_general(
                q_ref[h, a : a + query_rows, :], k_ref[h, n : n + span, :], (((1,), (1,)), ((), ())),
                preferred_element_type=F32,
            )
            if bias is not None:
                s = s + bias[:, n - at : n - at + span]
            buffers[unit % 2][:, n : n + span] = s
            for m in range(0, span, fold):
                state = jnp.maximum(state, s[:, m : m + fold])
        return state

    fresh = jnp.full((query_rows, fold), -3e38, F32)
    state = fresh
    for part in parts:
        state = score(0, state, part)
    for unit, (h, a) in enumerate(units):
        top = jnp.max(state, axis=1, keepdims=True)
        state = fresh
        total = jnp.zeros((query_rows, fold), F32)
        weighted = jnp.zeros((query_rows, size), F32)
        for part in parts:
            at, length, _ = part
            soft = jnp.exp2((buffers[unit % 2][:, at : at + length] - top) * scale)
            for m in range(0, length, fold):
                total = total + soft[:, m : m + fold]
            weighted = weighted + dot(soft.astype(BF16), v_ref[h, at : at + length, :])
            if unit + 1 < len(units):
                state = score(unit + 1, state, part)
        out_ref[a : a + query_rows, h * size : (h + 1) * size] = (
            weighted / jnp.sum(total, axis=1, keepdims=True)
        ).astype(BF16)
    part = 2 * cells
    for t in range(frames):
        base = t * 4 * cells
        own_ref[t * part : (t + 1) * part, :] = out_ref[base : base + part, :]
        sib_ref[t * part : (t + 1) * part, :] = out_ref[base + part : base + 2 * part, :]


def combine_local_kernel(own_ref, sib_ref, w_local_ref, total_ref):
    core = lax.axis_index("seq") % 2
    depth = own_ref.shape[1]
    mine = pl.ds(pl.multiple_of(core * depth, depth), depth)
    other = pl.ds(pl.multiple_of((1 - core) * depth, depth), depth)
    step = 512
    for n in range(0, total_ref.shape[1], step):
        columns = slice(n, n + step)
        total = dot(own_ref[...], w_local_ref[mine, columns])
        total_ref[:, columns] = total + dot(sib_ref[...], w_local_ref[other, columns])


def combine_kernel(total_ref, across_ref, corner_ref, w_across_ref, w_corner_ref, out_ref, held_ref, semaphores):
    step = 512
    copies = []
    for number, n in enumerate(range(0, held_ref.shape[1], step)):
        columns = slice(n, n + step)
        total = total_ref[:, columns] + dot(across_ref[...], w_across_ref[:, columns])
        total = total + dot(corner_ref[...], w_corner_ref[:, columns])
        held_ref[:, columns] = total.astype(BF16)
        copies.append(
            pltpu.make_async_copy(held_ref.at[:, columns], out_ref.at[:, columns], semaphores.at[number])
        )
        copies[-1].start()
    for copy in copies:
        copy.wait()


def in_hbm(*values):
    return [pltpu.with_memory_space_constraint(value, pltpu.HBM) for value in values]


def flip(value, mask, seq_count):
    pairs = [(i, i ^ mask) for i in range(2 * seq_count)]
    return lax.ppermute(value, ("grp", "seq"), pairs)


def local(
    feats, conv_weight, conv_bias, latent_projection_weight, noise, step_index, hist, hist_level,
    hist_count, w_in, w_hist, norm_gain, w_query, w_key, w_value, q_gain, k_gain, w_out,
):
    frame_count, channels, pixels = feats.shape
    seq_count = lax.axis_size("seq")
    group = lax.axis_index("grp")
    place = lax.axis_index("seq")
    core = place % 2
    width = w_in.shape[1]
    patch = w_in.shape[0]
    cells = pixels // 4
    slots = hist.shape[0]
    block = cells + 16
    lanes = frame_count * patch
    size = q_gain.shape[0]
    heads = w_query.shape[1] // size // 2
    depth = heads * size

    swapped = feats.transpose(0, 2, 1)
    earlier = lax.ppermute(swapped, "seq", [(i, i + 1) for i in range(seq_count - 1)])
    cos, sin = time_embed(step_index, width)
    wide, gram, partial, taps, latent, held_noise, tail = pl.pallas_call(
        prepare_kernel,
        out_shape=[
            jax.ShapeDtypeStruct((lanes, width), BF16),
            jax.ShapeDtypeStruct((3 * lanes, lanes), BF16),
            jax.ShapeDtypeStruct(swapped.shape, F32),
            jax.ShapeDtypeStruct((conv_weight.shape[0] - 1,) + conv_weight.shape[1:], BF16),
            jax.ShapeDtypeStruct(latent_projection_weight.shape, BF16),
            jax.ShapeDtypeStruct(noise.shape, BF16),
            jax.ShapeDtypeStruct((block - cells, lanes), BF16),
        ],
        in_specs=[VMEM] * 10,
        out_specs=[VMEM] * 7,
        compiler_params=pltpu.CompilerParams(vmem_limit_bytes=10 * 2**20),
        name="prepare",
    )(
        *in_hbm(
            w_in, cos, sin, swapped, conv_weight, conv_bias.reshape(1, channels),
            latent_projection_weight, noise, hist, hist_level.reshape(1, slots),
        )
    )
    earlier, partial = lax.optimization_barrier((earlier, partial))
    gathered = pl.pallas_call(
        encode_kernel,
        out_shape=jax.ShapeDtypeStruct((block, lanes), BF16),
        in_specs=[SMEM] + [VMEM] * 6,
        out_specs=VMEM,
        compiler_params=pltpu.CompilerParams(vmem_limit_bytes=6 * 2**20),
        name="encode",
    )(step_index, earlier, partial, taps, latent, held_noise, tail)
    columns = w_out.shape[1] // 2
    w_send = lax.dynamic_slice(w_out, (core * depth, (1 - group) * columns), (depth, columns))

    folded, w_v = pl.pallas_call(
        fold_kernel,
        out_shape=[
            jax.ShapeDtypeStruct((3 * lanes, depth), BF16), jax.ShapeDtypeStruct((width, depth), BF16)
        ],
        in_specs=[VMEM] * 2 + [pl.BlockSpec(memory_space=pltpu.HBM)],
        out_specs=[VMEM] * 2,
        scratch_shapes=[pltpu.SemaphoreType.DMA],
        compiler_params=pltpu.CompilerParams(vmem_limit_bytes=10 * 2**20),
        name="fold",
    )(wide, norm_gain.reshape(1, width), *in_hbm(w_value))
    bits = []
    bit = seq_count // 2
    while bit > 1:
        bits.append(bit)
        bit //= 2
    owner_masks = [0]
    for bit in bits:
        owner_masks = owner_masks + [m ^ bit for m in owner_masks]
    owner_masks = tuple(owner_masks + [m ^ 1 for m in owner_masks])
    bits.append(seq_count)
    rounds = [bits[i : i + 2] for i in range(len(bits) % 2, len(bits), 2)]
    if len(bits) % 2:
        rounds = [bits[:1]] + rounds
    for number, pair in enumerate(rounds):
        masks = [0] + [pair[0]] + ([pair[1], pair[0] ^ pair[1]] if len(pair) > 1 else [])
        near = [gathered]
        for mask in masks[1:]:
            near.append(flip(gathered, mask, seq_count))
        if number + 1 < len(rounds):
            gathered = jnp.concatenate(near, axis=0)
            gathered, w_send, folded = lax.optimization_barrier((gathered, w_send, folded))
    far = [flip(near[0], 1, seq_count)]
    far += [flip(piece, 1, seq_count) for piece in near[1:]]

    w_across = flip(w_send, seq_count, seq_count)
    w_local = lax.dynamic_slice_in_dim(w_out, group * columns, columns, axis=1)

    tokens = 2 * seq_count * frame_count * cells
    keys = tokens + slots * seq_count
    rows = frame_count * 4 * cells
    tile = 2 * rows
    query_rows = rows
    while 2 * query_rows * keys * 4 > 12 * 2**20:
        query_rows //= 2
    limit = (
        2 * tokens * lanes + 4 * width * depth + 4 * tile * width + 4 * keys * depth
        + 8 * query_rows * keys + 512 * width + 4 * rows * depth + 12 * 2**20
    )
    anywhere = pl.BlockSpec(memory_space=pltpu.HBM)
    own, sib = pl.pallas_call(
        functools.partial(
            joint_kernel, cells=cells, block=block, pieces=len(near), owner_masks=owner_masks, tile=tile,
            query_rows=query_rows,
        ),
        out_shape=[jax.ShapeDtypeStruct((rows // 2, depth), BF16)] * 2,
        in_specs=[VMEM] * (2 * len(near)) + [SMEM] + [VMEM] * 6 + [anywhere] * 2 + [VMEM] * 3,
        out_specs=[VMEM] * 2,
        scratch_shapes=[
            pltpu.VMEM((tokens, lanes), BF16),
            pltpu.VMEM((width, depth), BF16),
            pltpu.VMEM((width, depth), BF16),
            pltpu.VMEM((tile, width), BF16),
            pltpu.VMEM((tile, width), BF16),
            pltpu.VMEM((heads, rows, size), BF16),
            pltpu.VMEM((heads, keys, size), BF16),
            pltpu.VMEM((heads, keys, size), BF16),
            pltpu.VMEM((query_rows, keys), F32),
            pltpu.VMEM((query_rows, keys), F32),
            pltpu.VMEM((128, width), F32),
            pltpu.VMEM((rows, depth), BF16),
            pltpu.SemaphoreType.DMA((2,)),
        ],
        compiler_params=pltpu.CompilerParams(vmem_limit_bytes=limit),
        cost_estimate=pl.CostEstimate(
            flops=2 * keys * width * 3 * depth + 4 * rows * keys * depth,
            bytes_accessed=6 * width * depth,
            transcendentals=rows * keys * heads,
        ),
        name="joint",
    )(
        *near, *far, hist_count, wide, gram, folded, w_v, w_hist, norm_gain.reshape(1, width),
        *in_hbm(w_query, w_key), q_gain.reshape(1, size), k_gain.reshape(1, size), hist,
    )
    w_across, own, sib = lax.optimization_barrier((w_across, own, sib))
    w_corner = flip(w_across, 1, seq_count)
    from_sib = flip(sib, 1, seq_count)
    across = flip(own, seq_count, seq_count)
    corner = flip(sib, seq_count + 1, seq_count)
    total = pl.pallas_call(
        combine_local_kernel,
        out_shape=jax.ShapeDtypeStruct((rows // 2, columns), F32),
        in_specs=[VMEM] * 3,
        out_specs=VMEM,
        compiler_params=pltpu.CompilerParams(vmem_limit_bytes=10 * 2**20),
        name="combine_local",
    )(own, from_sib, w_local)
    return pl.pallas_call(
        combine_kernel,
        out_shape=jax.ShapeDtypeStruct((rows // 2, columns), BF16),
        in_specs=[VMEM] * 5,
        out_specs=anywhere,
        scratch_shapes=[
            pltpu.VMEM((rows // 2, columns), BF16), pltpu.SemaphoreType.DMA((columns // 512,))
        ],
        compiler_params=pltpu.CompilerParams(vmem_limit_bytes=10 * 2**20),
        name="combine",
    )(total, across, corner, w_across, w_corner)


def solution(mesh):
    placed = (
        P("seq", None, "grp"), P(), P(), P(), P("seq", None, "grp"), P(), P("seq", None), P("seq"),
        P(), P(), P(), P(), P(None, "grp"), P(None, "grp"), P(None, "grp"), P(), P(), P("grp", None),
    )
    return jax.shard_map(local, mesh=mesh, in_specs=placed, out_specs=P("seq", "grp"), check_vma=False)
```

```python
import functools
import math

import jax
import jax.numpy as jnp
from jax import lax
from jax.experimental import pallas as pl
from jax.experimental.pallas import tpu as pltpu
from jax.sharding import PartitionSpec as P


STEPS = 50
EPSILON = 1e-06
F32 = jnp.float32
BF16 = jnp.bfloat16
VMEM = pl.BlockSpec(memory_space=pltpu.VMEM)
SMEM = pl.BlockSpec(memory_space=pltpu.SMEM)


def dot(a, b):
    return jnp.dot(a, b, preferred_element_type=F32)


def dot_rows(a, b):
    return lax.dot_general(a, b, (((1,), (1,)), ((), ())), preferred_element_type=F32)


def time_embed(step_index, width):
    half_width = width // 2
    frequency = jnp.exp(-math.log(10000.0) * jnp.arange(half_width, dtype=F32) / half_width)
    angles = (step_index[0].astype(F32) * frequency).reshape(1, half_width)
    return jnp.cos(angles), jnp.sin(angles)


def column_of(row):
    count = row.shape[1]
    diagonal = lax.broadcasted_iota(jnp.int32, (count, count), 0) == lax.broadcasted_iota(
        jnp.int32, (count, count), 1
    )
    return jnp.sum(jnp.where(diagonal, row.astype(F32), 0.0), axis=1, keepdims=True)


def encode_kernel(step_ref, earlier_ref, partial_ref, weight_ref, latent_ref, noise_ref, tail_ref, out_ref):
    frames, pixels, _ = partial_ref.shape
    lat = noise_ref.shape[1]
    patch = lat * 4
    cells = pixels // 4
    taps = weight_ref.shape[0] + 1
    step = jnp.full((lat, pixels), step_ref[0].astype(F32), F32)
    sigma = (STEPS - step) / STEPS
    row = lax.broadcasted_iota(jnp.int32, (lat, frames * patch), 0)
    lane = lax.broadcasted_iota(jnp.int32, (lat, frames * patch), 1)
    pixel = lax.broadcasted_iota(jnp.int32, (pixels, frames * patch), 0)
    feature = lax.broadcasted_iota(jnp.int32, (pixels, frames * patch), 1)
    keep = (pixel % 4) == (feature % 4)
    collect = (
        lax.broadcasted_iota(jnp.int32, (cells, pixels), 1) // 4
        == lax.broadcasted_iota(jnp.int32, (cells, pixels), 0)
    ).astype(BF16)
    patches = jnp.zeros((cells, frames * patch), F32)
    for t in range(frames):
        total = partial_ref[t]
        for tap in range(t + 1, taps):
            total = total + dot_rows(earlier_ref[frames + t - tap], weight_ref[tap - 1])
        hidden = (total / (1.0 + jnp.exp(-total))).astype(BF16)
        mixed = dot_rows(latent_ref[...], hidden)
        noisy = ((1.0 - sigma) * mixed + sigma * noise_ref[t].astype(F32)).astype(BF16)
        spread = (lane // 4 == row + t * lat).astype(BF16)
        wide = lax.dot_general(noisy, spread, (((0,), (0,)), ((), ())), preferred_element_type=F32)
        wide = jnp.where(keep, wide, 0.0).astype(BF16)
        patches = patches + dot(collect, wide)
    out_ref[0:cells, :] = patches.astype(BF16)
    out_ref[cells:, :] = tail_ref[...]


def exact_parts(values):
    high = values.astype(BF16)
    rest = values - high.astype(F32)
    middle = rest.astype(BF16)
    return high, middle, (rest - middle.astype(F32)).astype(BF16)


def prepare_kernel(
    w_in_ref, cos_ref, sin_ref, feats_ref, weight_ref, bias_ref, latent_ref, noise_ref, hist_ref, level_ref,
    wide_ref, gram_ref, partial_ref, taps_ref, latent_out_ref, noise_out_ref, tail_ref,
):
    frames, pixels, channels = feats_ref.shape
    for t in range(frames):
        total = jnp.broadcast_to(bias_ref[...], (pixels, channels))
        for tap in range(t + 1):
            total = total + dot_rows(feats_ref[t - tap], weight_ref[tap])
        partial_ref[t] = total
    taps_ref[...] = weight_ref[1:]
    latent_out_ref[...] = latent_ref[...]
    noise_out_ref[...] = noise_ref[...]
    patch, width = w_in_ref.shape
    slots = hist_ref.shape[0]
    level = jnp.broadcast_to(column_of(level_ref[...]), (slots, patch))
    tail = jnp.concatenate([hist_ref[...].astype(F32), level], axis=1)
    rest = jnp.zeros((tail_ref.shape[0] - slots, 2 * patch), F32)
    tail_ref[...] = jnp.concatenate([tail, rest], axis=0).astype(BF16)
    lanes = wide_ref.shape[0]
    for n, source in ((0, cos_ref), (width // 2, sin_ref)):
        values = source[...]
        row = lax.broadcasted_iota(jnp.int32, (lanes - patch, values.shape[1]), 0)
        high, middle, low = exact_parts(values)
        extra = jnp.where(row == 0, high.astype(F32), 0.0)
        extra = jnp.where(row == 1, middle.astype(F32), extra)
        extra = jnp.where(row == 2, low.astype(F32), extra)
        wide_ref[patch:lanes, n : n + values.shape[1]] = extra.astype(BF16)
    wide_ref[0:patch, :] = w_in_ref[...]
    gram = jnp.zeros((lanes, lanes), F32)
    step = 512
    for n in range(0, width, step):
        part = wide_ref[:, n : n + step]
        gram = gram + dot_rows(part, part)
    for number, part in enumerate(exact_parts(gram)):
        gram_ref[number * lanes : (number + 1) * lanes, :] = part


def fold_kernel(wide_ref, gram_ref, gain_ref, w_value_ref, folded_ref, w_v_ref, semaphore):
    depth = w_v_ref.shape[1]
    lanes, width = wide_ref.shape
    folded_ref[:, 0:lanes] = gram_ref[...]
    start = pl.multiple_of((lax.axis_index("seq") % 2) * depth, depth)
    copy = pltpu.make_async_copy(w_value_ref.at[:, pl.ds(start, depth)], w_v_ref, semaphore)
    copy.start()
    copy.wait()
    total = jnp.zeros((lanes, depth), F32)
    step = 512
    for n in range(0, width, step):
        values = wide_ref[:, n : n + step].astype(F32) * gain_ref[:, n : n + step]
        stacked = jnp.concatenate(exact_parts(values), axis=0)
        product = dot(stacked, w_v_ref[n : n + step, :])
        total = total + (product[0:lanes] + (product[lanes : 2 * lanes] + product[2 * lanes :]))
    for number, part in enumerate(exact_parts(total)):
        folded_ref[number * lanes : (number + 1) * lanes, lanes:] = part


def joint_kernel(*refs, frames, cells, block, pieces, owner_masks, tile, query_rows):
    near, far = refs[:pieces], refs[pieces : 2 * pieces]
    (
        count_ref, wide_ref, folded_ref, w_v_ref, w_hist_ref, gain_ref, w_query_ref, w_key_ref,
        q_gain_ref, k_gain_ref, hist_ref, own_ref, sib_ref,
        patch_ref, w_q_ref, w_k_ref, tok_a_ref, tok_b_ref, q_ref, k_ref, v_ref, s_a_ref,
        s_b_ref, x_ref, out_ref, semaphores,
    ) = refs[2 * pieces :]
    heads, _, size = k_ref.shape
    width = w_hist_ref.shape[1]
    depth = heads * size
    lanes = near[0].shape[1]
    patch = lanes // frames
    levels = w_hist_ref.shape[0] // patch
    rows = 4 * cells * frames
    group = lax.axis_index("grp")
    place = lax.axis_index("seq")
    start = pl.multiple_of((place % 2) * depth, depth)
    copies = [
        pltpu.make_async_copy(w_query_ref.at[:, pl.ds(start, depth)], w_q_ref, semaphores.at[0]),
        pltpu.make_async_copy(w_key_ref.at[:, pl.ds(start, depth)], w_k_ref, semaphores.at[1]),
    ]
    for copy in copies:
        copy.start()

    step = 512
    lane = lax.broadcasted_iota(jnp.int32, (1, lanes), 1)
    ones = jnp.where(lane < patch + 3, 1.0, 0.0)
    held = near[0].shape[0] // block
    half = pieces * held
    fours = []
    for sources in (near, far):
        mine = sources[0][0:cells, :]
        theirs = sources[pieces // 2][0:cells, :]
        fours.append(jnp.where(group == 0, mine, theirs))
        fours.append(jnp.where(group == 0, theirs, mine))
    for sources in (near, far):
        for p in range(half):
            if p != 0 and p != half // 2:
                fours.append((sources[p // held], (p % held) * block))
    for spot, item in enumerate(fours):
        values = (item[0][item[1] : item[1] + cells, :] if isinstance(item, tuple) else item).astype(F32)
        for t in range(frames):
            moved = values if t == 0 else pltpu.roll(values, lanes - t * patch, 1)
            at = (spot // 4) * rows + t * 4 * cells + (spot % 4) * cells
            patch_ref[at : at + cells, :] = jnp.where(lane < patch, moved, ones).astype(BF16)

    def store_values(values, at):
        for h in range(heads):
            v_ref[h, pl.ds(at, values.shape[0]), :] = values[:, h * size : (h + 1) * size].astype(BF16)

    def tokens_of(i, tok_ref):
        source = patch_ref[pl.ds(pl.multiple_of(i * tile, tile), tile), :]
        tripled = jnp.concatenate([source] * 3, axis=1)
        products = dot(tripled, folded_ref[...])
        mean = jnp.sum(products[:, 0:lanes] * source.astype(F32), axis=1, keepdims=True) / width
        inverse = lax.rsqrt(mean + EPSILON)
        store_values(products[:, lanes:] * inverse, pl.multiple_of(i * tile, tile))
        for n in range(0, width, step):
            x = dot(source, wide_ref[:, n : n + step])
            tok_ref[:, n : n + step] = (x * inverse * gain_ref[:, n : n + step]).astype(BF16)

    def head_norm(values, gain):
        mean = jnp.mean(values * values, axis=1, keepdims=True)
        return (values * lax.rsqrt(mean + EPSILON) * gain).astype(BF16)

    def project(tokens, at):
        found = dot(tokens, w_k_ref[...])
        for h in range(heads):
            k_ref[h, pl.ds(at, tokens.shape[0]), :] = head_norm(
                found[:, h * size : (h + 1) * size], k_gain_ref[...]
            )

    tokens_of(0, tok_a_ref)
    for copy in copies:
        copy.wait()
    q = dot(tok_a_ref[0:rows, :], w_q_ref[...])
    for h in range(heads):
        q_ref[h] = head_norm(q[:, h * size : (h + 1) * size], q_gain_ref[...])
    tiles = patch_ref.shape[0] // tile

    def pair(j, carry):
        tokens_of(2 * j + 1, tok_b_ref)
        project(tok_a_ref[...], pl.multiple_of(2 * j * tile, tile))
        tokens_of(2 * j + 2, tok_a_ref)
        project(tok_b_ref[...], pl.multiple_of((2 * j + 1) * tile, tile))
        return carry

    if tiles > 2:
        lax.fori_loop(0, tiles // 2 - 1, pair, 0)
    tokens_of(tiles - 1, tok_b_ref)
    project(tok_a_ref[...], (tiles - 2) * tile)
    project(tok_b_ref[...], (tiles - 1) * tile)

    section = tiles * tile
    slots = hist_ref.shape[0]
    owners = len(owner_masks)
    spread = 128 // slots
    owner_blocks = [
        (sources[p // held], (p % held) * block + cells) for sources in (near, far) for p in range(half // 2)
    ]
    biases = []
    for r in range(0, owners, spread):
        taken = owner_blocks[r : r + spread]
        source = jnp.concatenate([ref[at : at + 16, :].astype(F32)[0:slots] for ref, at in taken], axis=0)
        count = source.shape[0]
        values, level = source[:, 0:patch], source[:, patch : 2 * patch]
        spread_rows = jnp.concatenate(
            [jnp.where(level == v, values, 0.0).astype(BF16) for v in range(levels)], axis=1
        )
        squares = jnp.zeros((count, 128), F32)
        for n in range(0, width, step):
            x = dot(spread_rows, w_hist_ref[:, n : n + step])
            x_ref[0:count, n : n + step] = x
            for m in range(0, step, 128):
                squares = squares + x[:, m : m + 128] * x[:, m : m + 128]
        inverse = lax.rsqrt(jnp.sum(squares, axis=1, keepdims=True) / width + EPSILON)
        for n in range(0, width, step):
            tok_a_ref[0:count, n : n + step] = (
                x_ref[0:count, n : n + step] * inverse * gain_ref[:, n : n + step]
            ).astype(BF16)
        project(tok_a_ref[0:count, :], section + r * slots)
        store_values(dot(tok_a_ref[0:count, :], w_v_ref[...]), section + r * slots)
        slot = lax.broadcasted_iota(jnp.int32, (1, count), 1)
        live = jnp.zeros((1, count), jnp.int32)
        for o in range(len(taken)):
            live = jnp.where(slot // slots == o, count_ref[place ^ owner_masks[r + o]], live)
        biases.append(jnp.where(slot % slots < live, 0.0, -1e30))

    scale = math.log2(math.e) / math.sqrt(size)
    chunk = 512
    fold = 128
    parts = [(a, chunk, None) for a in range(0, section, chunk)]
    parts += [(section + r * spread * slots, b.shape[1], b) for r, b in enumerate(biases)]
    units = [(h, a) for h in range(heads) for a in range(0, rows, query_rows)]
    buffers = (s_a_ref, s_b_ref)

    def score(unit, state, part):
        h, a = units[unit]
        at, length, bias = part
        for n in range(at, at + length, 256):
            span = min(256, at + length - n)
            s = lax.dot_general(
                q_ref[h, a : a + query_rows, :], k_ref[h, n : n + span, :], (((1,), (1,)), ((), ())),
                preferred_element_type=F32,
            )
            if bias is not None:
                s = s + bias[:, n - at : n - at + span]
            buffers[unit % 2][:, n : n + span] = s
            for m in range(0, span, fold):
                state = jnp.maximum(state, s[:, m : m + fold])
        return state

    fresh = jnp.full((query_rows, fold), -3e38, F32)
    state = fresh
    for part in parts:
        state = score(0, state, part)
    for unit, (h, a) in enumerate(units):
        top = jnp.max(state, axis=1, keepdims=True)
        state = fresh
        total = jnp.zeros((query_rows, fold), F32)
        weighted = jnp.zeros((query_rows, size), F32)
        for part in parts:
            at, length, _ = part
            if unit + 1 < len(units):
                state = score(unit + 1, state, part)
            soft = jnp.exp2((buffers[unit % 2][:, at : at + length] - top) * scale)
            for m in range(0, length, fold):
                total = total + soft[:, m : m + fold]
            weighted = weighted + dot(soft.astype(BF16), v_ref[h, at : at + length, :])
        out_ref[a : a + query_rows, h * size : (h + 1) * size] = (
            weighted / jnp.sum(total, axis=1, keepdims=True)
        ).astype(BF16)
    part = 2 * cells
    for t in range(frames):
        base = t * 4 * cells
        own_ref[t * part : (t + 1) * part, :] = out_ref[base : base + part, :]
        sib_ref[t * part : (t + 1) * part, :] = out_ref[base + part : base + 2 * part, :]


def combine_local_kernel(own_ref, sib_ref, w_local_ref, total_ref):
    core = lax.axis_index("seq") % 2
    depth = own_ref.shape[1]
    mine = pl.ds(pl.multiple_of(core * depth, depth), depth)
    other = pl.ds(pl.multiple_of((1 - core) * depth, depth), depth)
    step = 512
    for n in range(0, total_ref.shape[1], step):
        columns = slice(n, n + step)
        total = dot(own_ref[...], w_local_ref[mine, columns])
        total_ref[:, columns] = total + dot(sib_ref[...], w_local_ref[other, columns])


def combine_kernel(total_ref, across_ref, corner_ref, w_across_ref, w_corner_ref, out_ref, held_ref, semaphores):
    step = 512
    copies = []
    for number, n in enumerate(range(0, held_ref.shape[1], step)):
        columns = slice(n, n + step)
        total = total_ref[:, columns] + dot(across_ref[...], w_across_ref[:, columns])
        total = total + dot(corner_ref[...], w_corner_ref[:, columns])
        held_ref[:, columns] = total.astype(BF16)
        copies.append(
            pltpu.make_async_copy(held_ref.at[:, columns], out_ref.at[:, columns], semaphores.at[number])
        )
        copies[-1].start()
    for copy in copies:
        copy.wait()


def in_hbm(*values):
    return [pltpu.with_memory_space_constraint(value, pltpu.HBM) for value in values]


def flip(value, mask, seq_count):
    pairs = [(i, i ^ mask) for i in range(2 * seq_count)]
    return lax.ppermute(value, ("grp", "seq"), pairs)


def local(
    feats, conv_weight, conv_bias, latent_projection_weight, noise, step_index, hist, hist_level,
    hist_count, w_in, w_hist, norm_gain, w_query, w_key, w_value, q_gain, k_gain, w_out,
):
    frame_count, channels, pixels = feats.shape
    seq_count = lax.axis_size("seq")
    group = lax.axis_index("grp")
    place = lax.axis_index("seq")
    core = place % 2
    width = w_in.shape[1]
    patch = w_in.shape[0]
    cells = pixels // 4
    slots = hist.shape[0]
    block = cells + 16
    lanes = frame_count * patch
    size = q_gain.shape[0]
    heads = w_query.shape[1] // size // 2
    depth = heads * size

    swapped = feats.transpose(0, 2, 1)
    earlier = lax.ppermute(swapped, "seq", [(i, i + 1) for i in range(seq_count - 1)])
    cos, sin = time_embed(step_index, width)
    wide, gram, partial, taps, latent, held_noise, tail = pl.pallas_call(
        prepare_kernel,
        out_shape=[
            jax.ShapeDtypeStruct((lanes, width), BF16),
            jax.ShapeDtypeStruct((3 * lanes, lanes), BF16),
            jax.ShapeDtypeStruct(swapped.shape, F32),
            jax.ShapeDtypeStruct((conv_weight.shape[0] - 1,) + conv_weight.shape[1:], BF16),
            jax.ShapeDtypeStruct(latent_projection_weight.shape, BF16),
            jax.ShapeDtypeStruct(noise.shape, BF16),
            jax.ShapeDtypeStruct((block - cells, lanes), BF16),
        ],
        in_specs=[VMEM] * 10,
        out_specs=[VMEM] * 7,
        compiler_params=pltpu.CompilerParams(vmem_limit_bytes=10 * 2**20),
        name="prepare",
    )(
        *in_hbm(
            w_in, cos, sin, swapped, conv_weight, conv_bias.reshape(1, channels),
            latent_projection_weight, noise, hist, hist_level.reshape(1, slots),
        )
    )
    earlier, partial = lax.optimization_barrier((earlier, partial))
    gathered = pl.pallas_call(
        encode_kernel,
        out_shape=jax.ShapeDtypeStruct((block, lanes), BF16),
        in_specs=[SMEM] + [VMEM] * 6,
        out_specs=VMEM,
        compiler_params=pltpu.CompilerParams(vmem_limit_bytes=6 * 2**20),
        name="encode",
    )(step_index, earlier, partial, taps, latent, held_noise, tail)
    columns = w_out.shape[1] // 2
    w_send = lax.dynamic_slice(w_out, (core * depth, (1 - group) * columns), (depth, columns))

    folded, w_v = pl.pallas_call(
        fold_kernel,
        out_shape=[
            jax.ShapeDtypeStruct((3 * lanes, lanes + depth), BF16), jax.ShapeDtypeStruct((width, depth), BF16)
        ],
        in_specs=[VMEM] * 3 + [pl.BlockSpec(memory_space=pltpu.HBM)],
        out_specs=[VMEM] * 2,
        scratch_shapes=[pltpu.SemaphoreType.DMA],
        compiler_params=pltpu.CompilerParams(vmem_limit_bytes=10 * 2**20),
        name="fold",
    )(wide, gram, norm_gain.reshape(1, width), *in_hbm(w_value))
    bits = []
    bit = seq_count // 2
    while bit > 1:
        bits.append(bit)
        bit //= 2
    owner_masks = [0]
    for bit in bits:
        owner_masks = owner_masks + [m ^ bit for m in owner_masks]
    owner_masks = tuple(owner_masks + [m ^ 1 for m in owner_masks])
    bits.append(seq_count)
    rounds = [bits[i : i + 2] for i in range(len(bits) % 2, len(bits), 2)]
    if len(bits) % 2:
        rounds = [bits[:1]] + rounds
    for number, pair in enumerate(rounds):
        masks = [0] + [pair[0]] + ([pair[1], pair[0] ^ pair[1]] if len(pair) > 1 else [])
        near = [gathered]
        for mask in masks[1:]:
            near.append(flip(gathered, mask, seq_count))
        if number + 1 < len(rounds):
            gathered = jnp.concatenate(near, axis=0)
            gathered, w_send, folded = lax.optimization_barrier((gathered, w_send, folded))
    far = [flip(near[0], 1, seq_count)]
    far += [flip(piece, 1, seq_count) for piece in near[1:]]

    w_across = flip(w_send, seq_count, seq_count)
    w_local = lax.dynamic_slice_in_dim(w_out, group * columns, columns, axis=1)

    tokens = 2 * seq_count * frame_count * cells
    keys = tokens + slots * seq_count
    rows = frame_count * 4 * cells
    tile = 2 * rows
    query_rows = rows
    while 2 * query_rows * keys * 4 > 12 * 2**20:
        query_rows //= 2
    limit = (
        2 * tokens * lanes + 4 * width * depth + 4 * tile * width + 4 * keys * depth
        + 8 * query_rows * keys + 512 * width + 4 * rows * depth + 12 * 2**20
    )
    anywhere = pl.BlockSpec(memory_space=pltpu.HBM)
    own, sib = pl.pallas_call(
        functools.partial(
            joint_kernel, frames=frame_count, cells=cells, block=block, pieces=len(near), owner_masks=owner_masks, tile=tile,
            query_rows=query_rows,
        ),
        out_shape=[jax.ShapeDtypeStruct((rows // 2, depth), BF16)] * 2,
        in_specs=[VMEM] * (2 * len(near)) + [SMEM] + [VMEM] * 5 + [anywhere] * 2 + [VMEM] * 3,
        out_specs=[VMEM] * 2,
        scratch_shapes=[
            pltpu.VMEM((tokens, lanes), BF16),
            pltpu.VMEM((width, depth), BF16),
            pltpu.VMEM((width, depth), BF16),
            pltpu.VMEM((tile, width), BF16),
            pltpu.VMEM((tile, width), BF16),
            pltpu.VMEM((heads, rows, size), BF16),
            pltpu.VMEM((heads, keys, size), BF16),
            pltpu.VMEM((heads, keys, size), BF16),
            pltpu.VMEM((query_rows, keys), F32),
            pltpu.VMEM((query_rows, keys), F32),
            pltpu.VMEM((128, width), F32),
            pltpu.VMEM((rows, depth), BF16),
            pltpu.SemaphoreType.DMA((2,)),
        ],
        compiler_params=pltpu.CompilerParams(vmem_limit_bytes=limit),
        cost_estimate=pl.CostEstimate(
            flops=2 * keys * width * 3 * depth + 4 * rows * keys * depth,
            bytes_accessed=6 * width * depth,
            transcendentals=rows * keys * heads,
        ),
        name="joint",
    )(
        *near, *far, hist_count, wide, folded, w_v, w_hist.reshape(-1, width), norm_gain.reshape(1, width),
        *in_hbm(w_query, w_key), q_gain.reshape(1, size), k_gain.reshape(1, size), hist,
    )
    w_across, own, sib = lax.optimization_barrier((w_across, own, sib))
    w_corner = flip(w_across, 1, seq_count)
    from_sib = flip(sib, 1, seq_count)
    across = flip(own, seq_count, seq_count)
    corner = flip(sib, seq_count + 1, seq_count)
    total = pl.pallas_call(
        combine_local_kernel,
        out_shape=jax.ShapeDtypeStruct((rows // 2, columns), F32),
        in_specs=[VMEM] * 3,
        out_specs=VMEM,
        compiler_params=pltpu.CompilerParams(vmem_limit_bytes=10 * 2**20),
        name="combine_local",
    )(own, from_sib, w_local)
    return pl.pallas_call(
        combine_kernel,
        out_shape=jax.ShapeDtypeStruct((rows // 2, columns), BF16),
        in_specs=[VMEM] * 5,
        out_specs=anywhere,
        scratch_shapes=[
            pltpu.VMEM((rows // 2, columns), BF16), pltpu.SemaphoreType.DMA((columns // 512,))
        ],
        compiler_params=pltpu.CompilerParams(vmem_limit_bytes=10 * 2**20),
        name="combine",
    )(total, across, corner, w_across, w_corner)


def solution(mesh):
    placed = (
        P("seq", None, "grp"), P(), P(), P(), P("seq", None, "grp"), P(), P("seq", None), P("seq"),
        P(), P(), P(), P(), P(None, "grp"), P(None, "grp"), P(None, "grp"), P(), P(), P("grp", None),
    )
    return jax.shard_map(local, mesh=mesh, in_specs=placed, out_specs=P("seq", "grp"), check_vma=False)
```
